128 devices in a mesh: px: 8 (over x, core), py: 16 (over y, z).
Axes of the slice: x: 4, y: 4, z: 4, core: 2. Of those that a mesh axis runs over, the one named last changes fastest.
Arguments:
- potential: float32 [256, 256, 256], P('px', 'py'), may hold values from -2.4 to 2.4
- owner: int32 [8, 16, 256, 1], P('px', 'py'), may hold values from 0 to 127; in each aligned block of 256 rows (0 to 255, 256 to 511, ..., all dimensions but the last counted through in order) at most 4 rows name the same one
- window: int32 [8, 16, 256], P('px', 'py'), may hold values from 0 to 255
Outputs:
- displacement: float32 [3, 256, 256, 256], P(None, 'px', 'py')
- density: float32 [256, 256, 256], P('px', 'py')
The draws below stay inside these ranges and needn't reach their ends.
Inputs may be any that keep to these rules, and one draw needn't show every extreme that they name: Among the 256 blocks of one tile (i, j), no owner is named more than 4 times, and the bound 4 is reached.
All inputs are finite; a program needn't handle non-finite values.
Results may differ from the reference program's by a relative error of at most 0.0003.
Values sent between devices are 32-bit elements; how exact they have to be, the bound alone decides.
A program may use at most 128 MiB of HBM per device.

```python
import math
import jax
import jax.numpy as jnp
import numpy as np
from jax import lax

CX = 32
CY = 16
NZ = 256
TILES_X = 8
TILES_Y = 16
NX = 256
NY = 256
BX = 4
BY = 2
BZ = 32
NBLK = 256
CAP = 4


def plant(entries, own_key, smallest, top_value):
    longest = entries.shape.index(max(entries.shape))
    spots = []
    for shift in (0, 1):
        where = [jax.random.randint(jax.random.fold_in(own_key, axis), (), 0, length) for axis, length in enumerate(entries.shape)]
        where[longest] = (where[longest] + shift) % entries.shape[longest]
        spots.append(tuple(where))
    return entries.at[spots[0]].set(smallest).at[spots[1]].set(top_value)


def levels(own_key, extent, cuts, low, top_value):
    def one(position, shards_of):
        heights = jax.random.uniform(jax.random.fold_in(jax.random.fold_in(own_key, 6), position), (shards_of,), jnp.float32, low / len(cuts), top_value / len(cuts))
        return jnp.repeat(jnp.exp(heights), extent[position] // shards_of).reshape((-1,) + (1,) * (len(extent) - position - 1))

    gain = one(*cuts[0])
    for cut in cuts[1:]:
        gain = gain * one(*cut)
    return gain


def deal_out(rng, own, number, rows, number_of, top, bound, lean):
    sequence = jax.random.permutation(rng, number_of)
    packed, ordinary = load_shares(number_of, rows * top, bound, lean, True), load_shares(number_of, rows * top, bound, lean, False)
    places = jnp.arange(number_of)

    def named(lengths, rotation):
        used = int((lengths > 0).sum())
        fixed = max(1, used // 4)
        passed = fixed + (places - fixed + rotation * (used - fixed)) % max(1, number_of - fixed)
        return jnp.zeros((number_of,), jnp.int32).at[sequence[jnp.where(places < fixed, places, passed)]].set(jnp.asarray(lengths, jnp.int32))

    lengths = jnp.where(number % 4 == 0, named(packed, number // 4), named(ordinary, number - number // 4 - 1))
    mixed = jax.random.permutation(jax.random.fold_in(own, 3), number_of)
    source_of, receiver = mixed[0:number_of // 2 * 2:2], mixed[1:number_of // 2 * 2:2]
    margin = jnp.minimum(lengths[source_of] - 1, bound - lengths[receiver]) // 2
    margin = jnp.where((source_of == sequence[0]) | (receiver == sequence[0]) | (lengths[receiver] == 0), 0, jnp.maximum(margin, 0))
    passed = jax.random.randint(jax.random.fold_in(own, 4), (number_of // 2,), 0, 1 << 20) % (margin + 1)
    lengths = lengths.at[source_of].add(-passed).at[receiver].add(passed)
    labels = jnp.searchsorted(jnp.cumsum(lengths), jnp.arange(rows * top), side="right").astype(jnp.int32)
    table = labels.reshape(top, rows).T
    table = table[jax.random.permutation(jax.random.fold_in(own, 1), rows)]
    rotation = jax.random.randint(jax.random.fold_in(own, 2), (rows, 1), 0, top)
    return jnp.take_along_axis(table, (jnp.arange(top)[None, :] + rotation) % top, axis=1)


def load_shares(number_of, total, bound, skew, full):
    loads = [(1 << 20) // math.isqrt(standing ** skew) + 1 for standing in range(1, number_of + 1)]
    largest = bound if full else min(bound, max(-(-total // number_of), total * loads[0] // sum(loads)))
    least = 1 if total - largest >= number_of - 1 else 0
    given, spare = [largest] + [least] * (number_of - 1), total - largest - least * (number_of - 1)
    while spare > 0:
        free = [i for i in range(1, number_of) if given[i] < largest] or [i for i in range(1, number_of) if given[i] < bound]
        pool, remaining = sum([loads[i] for i in free]), spare
        for i in free:
            more = min(bound - given[i], max(1, remaining * loads[i] // pool), spare)
            given[i] = given[i] + more
            spare = spare - more
    return np.array(given)


def bell_draw(rng, shape, deviation, most, shards=(), held_as=jnp.bfloat16):
    drawn = jax.random.normal(rng, shape, jnp.float32) * deviation
    if len(shards) > 0:
        drawn = levels(rng, shape, shards, -0.22, 0.18) * drawn
    return jnp.clip(drawn, min=-most, max=most).astype(held_as)


def setup_inputs(seed: int = 0) -> dict:
    splits = jax.random.split(jax.random.key(seed), 4)
    potential = bell_draw(splits[0], (NX, NY, NZ), 0.4, 2.4, ((0, 8), (1, 16)), jnp.float32)
    owner_keys = jax.random.split(jax.random.fold_in(splits[1], 1), TILES_X * TILES_Y * NBLK // NBLK)
    owner_turns = jax.random.permutation(jax.random.fold_in(splits[1], 3), TILES_X * TILES_Y * NBLK // NBLK)
    owner = jax.vmap(lambda own, number: deal_out(jax.random.fold_in(splits[1], 2), own, number, NBLK, TILES_X * TILES_Y, 1, CAP, 2))(owner_keys, owner_turns).reshape((TILES_X, TILES_Y, NBLK, 1))
    window = plant(jax.random.randint(splits[2], (TILES_X, TILES_Y, NBLK), 0, NBLK), jax.random.fold_in(splits[2], 1), 0, NBLK - 1).astype(jnp.int32)
    return {"potential": potential, "owner": owner, "window": window}


SECOND_ORDER = 3.0 / 7.0
HIGHEST = lax.Precision.HIGHEST


def spline_weight(offset):
    magnitude = jnp.abs(offset)
    inner = (4.0 - 6.0 * magnitude * magnitude + 3.0 * magnitude * magnitude * magnitude) / 6.0
    reach = jnp.maximum(2.0 - magnitude, 0.0)
    outer = reach * reach * reach / 6.0
    return jnp.where(magnitude < 1.0, inner, outer)


def deposit_blocks(shifts):
    count = shifts.shape[0]
    within = jnp.arange(512)
    offsets = jnp.stack([within // 64, (within // 8) % 8, within % 8]).astype(jnp.float32)
    places = 2.0 + offsets[None] + shifts
    cells = jnp.arange(12).astype(jnp.float32)
    weights = spline_weight(cells[None, None, :, None] - places[:, :, None, :])
    planar = (weights[:, 0, :, None, :] * weights[:, 1, None, :, :]).reshape(count, 144, 512)
    windows = jnp.einsum('sqp,swp->sqw', planar, weights[:, 2], precision=HIGHEST)
    return windows.reshape(count, 1728)


def periodic_gradient(field, axis):
    return (jnp.roll(field, -1, axis) - jnp.roll(field, 1, axis)) * 0.5


def laplace_modes(length):
    modes = jnp.arange(length)
    return modes, 2.0 * jnp.cos(modes.astype(jnp.float32) * (2.0 * jnp.pi / length)) - 2.0


def reference(potential, owner, window):
    ahead_x = jnp.roll(potential, -1, 0)
    behind_x = jnp.roll(potential, 1, 0)
    ahead_y = jnp.roll(potential, -1, 1)
    behind_y = jnp.roll(potential, 1, 1)
    ahead_z = jnp.roll(potential, -1, 2)
    behind_z = jnp.roll(potential, 1, 2)
    curve_xx = ahead_x - 2.0 * potential + behind_x
    curve_yy = ahead_y - 2.0 * potential + behind_y
    curve_zz = ahead_z - 2.0 * potential + behind_z
    curve_xy = (jnp.roll(ahead_x, -1, 1) - jnp.roll(ahead_x, 1, 1) - jnp.roll(behind_x, -1, 1) + jnp.roll(behind_x, 1, 1)) * 0.25
    curve_xz = (jnp.roll(ahead_x, -1, 2) - jnp.roll(ahead_x, 1, 2) - jnp.roll(behind_x, -1, 2) + jnp.roll(behind_x, 1, 2)) * 0.25
    curve_yz = (jnp.roll(ahead_y, -1, 2) - jnp.roll(ahead_y, 1, 2) - jnp.roll(behind_y, -1, 2) + jnp.roll(behind_y, 1, 2)) * 0.25
    source = curve_xx * curve_yy + curve_xx * curve_zz + curve_yy * curve_zz - curve_xy * curve_xy - curve_xz * curve_xz - curve_yz * curve_yz
    modes_x, lap_x = laplace_modes(NX)
    modes_y, lap_y = laplace_modes(NY)
    modes_z, lap_z = laplace_modes(NZ)
    eigen = lap_x[:, None, None] + lap_y[None, :, None] + lap_z[None, None, :]
    anchor = (modes_x == 0)[:, None, None] & (modes_y == 0)[None, :, None] & (modes_z == 0)[None, None, :]
    inverse = jnp.where(anchor, 0.0, 1.0 / jnp.where(anchor, -1.0, eigen))
    spectrum = jnp.fft.fftn(source)
    second = jnp.real(jnp.fft.ifftn(spectrum * inverse))
    displacement = jnp.stack([-periodic_gradient(potential, component) - SECOND_ORDER * periodic_gradient(second, component) for component in range(3)])
    shift = jnp.clip(displacement, -1.0, 1.0)
    blocks = shift.reshape(3, TILES_X, BX, 8, TILES_Y, BY, 8, BZ, 8).transpose(1, 4, 2, 5, 7, 0, 3, 6, 8).reshape(TILES_X * TILES_Y, NBLK, 3, 512)
    owner_rows = owner.reshape(TILES_X * TILES_Y, NBLK)
    window_rows = window.reshape(TILES_X * TILES_Y, NBLK)
    span = jnp.arange(12).astype(jnp.int32)

    def add_tile(grid, items):
        shifts, owners, windows = items
        values = deposit_blocks(shifts).reshape(NBLK, 12, 12, 12)
        start_x = (owners // TILES_Y) * CX + 8 * (windows // (BY * BZ)) - 2
        start_y = (owners % TILES_Y) * CY + 8 * ((windows // BZ) % BY) - 2
        start_z = 8 * (windows % BZ) - 2
        index_x = (start_x[:, None] + span[None, :]) % NX
        index_y = (start_y[:, None] + span[None, :]) % NY
        index_z = (start_z[:, None] + span[None, :]) % NZ
        grid = grid.at[index_x[:, :, None, None], index_y[:, None, :, None], index_z[:, None, None, :]].add(values)
        return grid, None

    density, ignored = lax.scan(add_tile, jnp.zeros((NX, NY, NZ), jnp.float32), (blocks, owner_rows, window_rows))
    return displacement, density
```

```python
import functools
import math

import jax
import jax.numpy as jnp
import numpy as np
from jax import lax
from jax.experimental import pallas as pl
from jax.experimental.pallas import tpu as pltpu
from jax.sharding import PartitionSpec as P

SECOND_ORDER = 3.0 / 7.0
HIGHEST = lax.Precision.HIGHEST
F32 = jnp.float32
BF16 = jnp.bfloat16
N = 256
VLIM = 60 * 1024 * 1024


def cas_table(a, b):
    angle = (np.multiply.outer(a, b) % N) * (2.0 * math.pi / N)
    return np.cos(angle) + np.sin(angle)


def plane_rows():
    r = np.arange(512)
    xh, q, xl, i = r % 4, r // 4 % 2, r // 8 % 8, r // 64
    return 32 * i + 8 * xh + xl, q


def constants():
    n = np.arange(N)
    tz = cas_table(n, n).astype(np.float32)
    x, q = plane_rows()
    lxs = (cas_table(x, x) * (q[:, None] == q[None, :])).astype(np.float32)
    lap = -4.0 * np.sin(math.pi * n / N) ** 2
    return tz, lxs, lap[x][:, None].astype(np.float32), lap[None, :].astype(np.float32), lap.astype(np.float32)


def block_select():
    sel = np.zeros((640, 8, 128), np.float32)

    def cell(x, y):
        return x * 16 + y

    for bx in range(4):
        for by in range(2):
            g = bx * 2 + by
            for a in range(8):
                x = 8 * bx + a
                for c in range(8):
                    sel[cell(x, 8 * by + c), g, a * 8 + c] = 1.0
                sel[544 + x if by == 0 else cell(x, 7), g, 80 + a] = 1.0
                sel[cell(x, 8) if by == 0 else 576 + x, g, 88 + a] = 1.0
            for c in range(8):
                y = 8 * by + c
                sel[512 + y if bx == 0 else cell(8 * bx - 1, y), g, 64 + c] = 1.0
                sel[528 + y if bx == 3 else cell(8 * bx + 8, y), g, 72 + c] = 1.0
    return sel.reshape(640, 1024)


def spread_z():
    sel = np.zeros((12, 32, N), np.float32)
    for s in range(12):
        for b in range(32):
            sel[s, b, (8 * b + s - 2) % N] = 1.0
    return sel.reshape(384, N)


TZ, LXS, LAPX, LAPY, LAP = constants()
SELECT = block_select()
SPREAD = spread_z()


def lane_iota(shape):
    return lax.broadcasted_iota(jnp.int32, shape, len(shape) - 1)


def swap_groups(vals, width):
    count = len(vals)
    group = lane_iota(vals[0].shape) // width
    step = 1
    while step < count:
        low = (group & step) == 0
        new = list(vals)
        for k in range(count):
            if k & step:
                continue
            a, b = vals[k], vals[k + step]
            new[k] = jnp.where(low, a, pltpu.roll(b, step * width, 1))
            new[k + step] = jnp.where(low, pltpu.roll(a, 128 - step * width, 1), b)
        vals = new
        step *= 2
    return vals


def split3(x):
    a = x.astype(BF16)
    r = x - a.astype(F32)
    b = r.astype(BF16)
    c = (r - b.astype(F32)).astype(BF16)
    return a, b, c


def split2(x):
    a = x.astype(BF16)
    return a, (x - a.astype(F32)).astype(BF16)


def bdot(a, b):
    return jnp.dot(a, b, preferred_element_type=F32)


def shift_rows(p, before, after):
    up = jnp.concatenate([p[1:], after], axis=0)
    down = jnp.concatenate([before, p[:-1]], axis=0)
    return up, down


def source_kernel(p_ref, xlo_ref, xhi_ref, ylo_ref, yhi_ref, tz_ref, out_ref, s_ref):
    planes = []
    for x in range(34):
        p = xlo_ref[...] if x == 0 else xhi_ref[...] if x == 33 else p_ref[x - 1]
        up, down = shift_rows(p, ylo_ref[x : x + 1, :], yhi_ref[x : x + 1, :])
        ahead, behind = pltpu.roll(p, N - 1, 1), pltpu.roll(p, 1, 1)
        planes.append((p, up - down, ahead - behind, up + down - 2.0 * p, ahead + behind - 2.0 * p))
        if x < 2:
            continue
        (p0, dy0, dz0, _, _), (p1, dy1, _, yy, zz), (p2, dy2, dz2, _, _) = planes[-3:]
        xx = p2 - 2.0 * p1 + p0
        xy, xz = dy2 - dy0, dz2 - dz0
        yz = pltpu.roll(dy1, N - 1, 1) - pltpu.roll(dy1, 1, 1)
        value = xx * (yy + zz) + yy * zz - (xy * xy + xz * xz + yz * yz) * 0.0625
        s_ref[16 * (x - 2) : 16 * (x - 1), :] = value
    for xh in range(4):
        part = s_ref[128 * xh : 128 * xh + 128, :]
        r = lax.dot_general(
            tz_ref[...], part, (((1,), (1,)), ((), ())), precision=HIGHEST, preferred_element_type=F32
        )
        out_ref[:, xh, :] = r[:128]
        out_ref[:, 4 + xh, :] = r[128:]


def solve_kernel(lz_ref, x_ref, lxs_ref, ty_ref, lapx_ref, lapy_ref, out_ref, m_ref):
    for i in range(8):
        for h in range(2):
            base = i * 16 + h * 8
            vals = swap_groups([x_ref[base + j] for j in range(8)], 16)
            for xl in range(8):
                m_ref[(i * 8 + xl) * 8 : (i * 8 + xl) * 8 + 8, h * 128 : h * 128 + 128] = vals[xl]
    hp = functools.partial(jnp.dot, precision=HIGHEST, preferred_element_type=F32)
    b = hp(lxs_ref[...], hp(m_ref[...], ty_ref[...]))
    first = lax.broadcasted_iota(jnp.int32, (512, 1), 0) // 4 % 2 == 0
    column = lapx_ref[...] + jnp.where(first, lz_ref[0, 0], lz_ref[0, 1])
    eigen = column + lapy_ref[...]
    anchor = eigen == 0.0
    scale = SECOND_ORDER / (N * N * N)
    b = b * jnp.where(anchor, 0.0, scale / jnp.where(anchor, -1.0, eigen))
    m_ref[...] = hp(hp(lxs_ref[...], b), ty_ref[...])
    for i in range(8):
        for h in range(2):
            base = i * 16 + h * 8
            vals = [
                m_ref[(i * 8 + xl) * 8 : (i * 8 + xl) * 8 + 8, h * 128 : h * 128 + 128] for xl in range(8)
            ]
            vals = swap_groups(vals, 16)
            for j in range(8):
                out_ref[base + j] = vals[j]


def back_kernel(x_ref, tz_ref, p_ref, out_ref):
    for xh in range(4):
        a = jnp.concatenate([x_ref[:, xh, :], x_ref[:, 4 + xh, :]], axis=0)
        r = jnp.dot(a.T, tz_ref[...], precision=HIGHEST, preferred_element_type=F32)
        out_ref[128 * xh : 128 * xh + 128, :] = p_ref[128 * xh : 128 * xh + 128, :] + r


def displace_kernel(f_ref, xlo_ref, xhi_ref, ylo_ref, yhi_ref, out_ref):
    for x in range(32):
        f = f_ref[x]
        before = xlo_ref[...] if x == 0 else f_ref[x - 1]
        after = xhi_ref[...] if x == 31 else f_ref[x + 1]
        up, down = shift_rows(f, ylo_ref[x : x + 1, :], yhi_ref[x : x + 1, :])
        out_ref[0, x] = (before - after) * 0.5
        out_ref[1, x] = (down - up) * 0.5
        out_ref[2, x] = (pltpu.roll(f, 1, 1) - pltpu.roll(f, N - 1, 1)) * 0.5


def dispatch_kernel(
    f_ref, xlo_ref, xhi_ref, ylo_ref, yhi_ref, sel_ref, orow_ref, ocol_ref, wcol_ref,
    o0_ref, o1_ref, o2_ref, o3_ref, ft_ref,
):
    for m in range(4):
        ft_ref[m] = f_ref[128 * m : 128 * m + 128, :].T
    faces = jnp.concatenate(
        [xlo_ref[...], xhi_ref[...], ylo_ref[...], yhi_ref[...], jnp.zeros((32, N), F32)], axis=0
    )
    ft_ref[4] = faces.T
    ordered = jnp.concatenate(
        [jnp.concatenate([ft_ref[m, pl.ds(e, 32, stride=8), :] for e in range(8)], axis=0) for m in range(5)],
        axis=1,
    )
    sel = sel_ref[...]
    a, b, c = split3(ordered)
    w = bdot(a, sel) + bdot(b, sel) + bdot(c, sel)

    def slab(e, turn):
        rows = w[32 * e : 32 * e + 32]
        if turn:
            rows = pltpu.roll(rows, turn, 0)
        return jnp.concatenate([rows[:, 128 * g : 128 * g + 128] for g in range(8)], axis=0)

    zfaces = (slab(7, 1), slab(0, 31))
    lanes = lane_iota((256, 128))
    slabs = []
    for e in range(8):
        v = slab(e, 0)
        face = pltpu.roll(zfaces[e // 4], 96 - 16 * (e % 4), 1)
        v = jnp.where((lanes >= 96) & (lanes < 112), face, v)
        if e == 0:
            v = jnp.where(lanes == 112, wcol_ref[...] + 1.0, v)
        slabs.append(v)
    orow, ocol = orow_ref[...], ocol_ref[...]
    r_i = lax.broadcasted_iota(jnp.int32, (256, 256), 0)
    c_i = lax.broadcasted_iota(jnp.int32, (256, 256), 1)
    same = jnp.where((ocol == orow) & (r_i < c_i), 1, 0)
    slot = jnp.sum(same, axis=0, keepdims=True) * 128 + orow
    hot = (lax.broadcasted_iota(jnp.int32, (512, 256), 0) == slot).astype(F32).astype(BF16)
    outs = (o0_ref, o1_ref, o2_ref, o3_ref)
    for e in range(0, 8, 2):
        a, b, c = split3(jnp.concatenate([slabs[e], slabs[e + 1]], axis=1))
        o = bdot(hot, a) + bdot(hot, b) + bdot(hot, c)
        for r in range(4):
            outs[r][:, e, :] = o[128 * r : 128 * r + 128, :128]
            outs[r][:, e + 1, :] = o[128 * r : 128 * r + 128, 128:]


def spline_taps(t):
    t = jnp.clip(t, -1.0, 1.0)
    up = jnp.maximum(t, 0.0)
    dn = up - t
    p3 = up * up * up * (1.0 / 6.0)
    n3 = dn * dn * dn * (1.0 / 6.0)
    sq = t * t
    both = p3 + n3
    base = sq * 0.5 + (1.0 / 6.0) - both
    half = t * 0.5
    return n3, base - half - 2.0 * n3, (2.0 / 3.0) - sq + 3.0 * both, base + half - 2.0 * p3, p3


def deposit_kernel(arr_ref, d_ref, lab_ref, c_ref, wx_ref, wy_ref, wz_ref, t_ref):
    lab_ref[...] = jnp.broadcast_to(arr_ref[:, 0, :][:, 112:113], (128, 128))
    for e in range(8):
        c_ref[128 * e : 128 * e + 128, :] = arr_ref[:, e, :].T
    sub = lax.broadcasted_iota(jnp.int32, (8, 128), 0)

    def cell(e, a):
        return c_ref[128 * e + 8 * a : 128 * e + 8 * a + 8, :]

    def zface(side, a):
        row = 128 * (4 * side + a // 2) + 96 + 8 * (a % 2)
        return c_ref[row : row + 8, :]

    for e in range(8):
        for a in range(8):
            f = cell(e, a)
            xm = cell(e, a - 1) if a > 0 else c_ref[128 * e + 64 : 128 * e + 72, :]
            xp = cell(e, a + 1) if a < 7 else c_ref[128 * e + 72 : 128 * e + 80, :]
            zm = cell(e - 1, a) if e > 0 else zface(0, a)
            zp = cell(e + 1, a) if e < 7 else zface(1, a)
            ym = jnp.broadcast_to(c_ref[128 * e + 80 + a : 128 * e + 81 + a, :], (8, 128))
            yp = jnp.broadcast_to(c_ref[128 * e + 88 + a : 128 * e + 89 + a, :], (8, 128))
            ym = jnp.where(sub == 0, ym, pltpu.roll(f, 1, 0))
            yp = jnp.where(sub == 7, yp, pltpu.roll(f, 7, 0))
            for ref, lo, hi in ((wx_ref, xm, xp), (wy_ref, ym, yp), (wz_ref, zm, zp)):
                for d, w in enumerate(spline_taps((lo - hi) * 0.5)):
                    ref[a, e, d] = w
    t_ref[...] = jnp.zeros_like(t_ref)

    def step(n, carry):
        a, dx = n // 5, n % 5
        u = a + dx
        acc = [[None] * 12 for _ in range(5)]
        for e in range(8):
            wx = wx_ref[a, e, dx]
            wz = [wz_ref[a, e, k] for k in range(5)]
            for dy in range(5):
                q = wx * wy_ref[a, e, dy]
                for dz in range(5):
                    v = q * wz[dz]
                    s = e + dz
                    acc[dy][s] = v if acc[dy][s] is None else acc[dy][s] + v
            for s in ([e] if e < 7 else range(7, 12)):
                for dy in range(5):
                    t_ref[u, s, dy] = t_ref[u, s, dy] + acc[dy][s]
        return carry

    lax.fori_loop(0, 40, step, 0)

    def fold(u, carry):
        for s in range(12):
            lo = t_ref[u, s, 0]
            hi = jnp.zeros((8, 128), F32)
            for dy in range(1, 5):
                turned = pltpu.roll(t_ref[u, s, dy], dy, 0)
                lo = lo + jnp.where(sub >= dy, turned, 0.0)
                hi = hi + jnp.where(sub >= dy, 0.0, turned)
            d_ref[s, u, 0:8, :] = lo
            d_ref[s, u, 8:16, :] = hi
        return carry

    lax.fori_loop(0, 12, fold, 0)


def gather_kernel(d0, d1, d2, d3, l0, l1, l2, l3, sp_ref, out_ref, g_ref, h_ref):
    ids = lane_iota((128, 256)).astype(F32) + 1.0
    hots = []
    for lab in (l0, l1, l2, l3):
        col = jnp.concatenate([lab[...], lab[...]], axis=1)
        hots.append((col == ids).astype(F32).astype(BF16))
    hot = jnp.concatenate(hots, axis=0)
    for s in range(12):
        d = jnp.concatenate([ref[s].reshape(192, 128) for ref in (d0, d1, d2, d3)], axis=1)
        a, b = split2(d)
        g_ref[s] = bdot(a, hot) + bdot(b, hot)
    for half in range(2):
        for k in range(3):
            vals = [g_ref[4 * k + m][:, 128 * half : 128 * half + 128] for m in range(4)]
            vals = swap_groups(vals, 32)
            for gl in range(4):
                h_ref[half * 4 + gl, :, 128 * k : 128 * k + 128] = vals[gl]
    out_ref[...] = jnp.zeros_like(out_ref)
    sp = sp_ref[...]
    for g in range(8):
        a, b = split2(h_ref[g])
        o = (bdot(a, sp) + bdot(b, sp)).reshape(12, 16, N)
        bx, by = g // 2, g % 2
        out_ref[8 * bx : 8 * bx + 12, 8 * by : 8 * by + 16, :] += o


def call(kernel, out_shape, scratch, smem=0, n_in=0):
    specs = [pl.BlockSpec(memory_space=pltpu.SMEM)] * smem
    specs += [pl.BlockSpec(memory_space=pltpu.VMEM)] * (n_in - smem)
    one = not isinstance(out_shape, (tuple, list))
    vm = pl.BlockSpec(memory_space=pltpu.VMEM)
    return pl.pallas_call(
        kernel,
        out_shape=out_shape,
        in_specs=specs,
        out_specs=vm if one else [vm] * len(out_shape),
        scratch_shapes=scratch,
        compiler_params=pltpu.CompilerParams(vmem_limit_bytes=VLIM),
    )


def sds(*shape):
    return jax.ShapeDtypeStruct(shape, F32)


def neighbour(x, axis, step):
    size = lax.axis_size(axis)
    return lax.ppermute(x, axis, [(i, (i + step) % size) for i in range(size)])


def exchange(x):
    return lax.all_to_all(x, ("px", "py"), split_axis=0, concat_axis=0, tiled=True)


def per_device(potential, owner, window):
    index = lax.axis_index("px") * 16 + lax.axis_index("py")
    lap = jnp.asarray(LAP)
    lz = jnp.stack([lap[index], lap[index + 128]]).reshape(1, 2)
    tz = jnp.asarray(TZ)
    lxs = jnp.asarray(LXS)
    sel = jnp.asarray(SELECT, BF16)
    spread = jnp.asarray(SPREAD, BF16)
    orow = owner.reshape(1, 256)
    ocol = owner.reshape(256, 1)
    wcol = window.reshape(256, 1).astype(F32)

    xlo = neighbour(potential[31], "px", 1)
    xhi = neighbour(potential[0], "px", -1)
    last = jnp.concatenate([xlo[15:16], potential[:, 15], xhi[15:16]], axis=0)
    lead = jnp.concatenate([xlo[0:1], potential[:, 0], xhi[0:1]], axis=0)
    ylo = neighbour(last, "py", 1)
    yhi = neighbour(lead, "py", -1)
    pieces = call(source_kernel, sds(128, 8, 128), [pltpu.VMEM((512, N), F32)], 0, 6)(
        potential, xlo, xhi, ylo, yhi, tz
    )
    planes = exchange(pieces)
    solved = call(solve_kernel, sds(128, 8, 128), [pltpu.VMEM((512, N), F32)], 1, 6)(
        lz, planes, lxs, tz, jnp.asarray(LAPX), jnp.asarray(LAPY)
    )
    returned = exchange(solved)
    flat = call(back_kernel, sds(512, N), [], 0, 3)(returned, tz, potential.reshape(512, N))
    total = flat.reshape(32, 16, N)
    fxlo = neighbour(total[31], "px", 1)
    fxhi = neighbour(total[0], "px", -1)
    fylo = neighbour(total[:, 15], "py", 1)
    fyhi = neighbour(total[:, 0], "py", -1)
    outgoing = call(dispatch_kernel, [sds(128, 8, 128)] * 4, [pltpu.VMEM((5, N, 128), F32)], 0, 9)(
        flat, fxlo, fxhi, fylo, fyhi, sel, orow, ocol, wcol
    )
    arrived = [exchange(o) for o in outgoing]
    displacement = call(displace_kernel, sds(3, 32, 16, N), [], 0, 5)(total, fxlo, fxhi, fylo, fyhi)
    parts, labels = [], []
    for a in arrived:
        d, lab = call(
            deposit_kernel,
            [sds(12, 12, 16, 128), sds(128, 128)],
            [
                pltpu.VMEM((1024, 128), F32),
                pltpu.VMEM((8, 8, 5, 8, 128), F32),
                pltpu.VMEM((8, 8, 5, 8, 128), F32),
                pltpu.VMEM((8, 8, 5, 8, 128), F32),
                pltpu.VMEM((12, 12, 5, 8, 128), F32),
            ],
            0,
            1,
        )(a)
        parts.append(d)
        labels.append(lab)
    tile = call(
        gather_kernel,
        sds(36, 24, N),
        [pltpu.VMEM((12, 192, N), F32), pltpu.VMEM((8, 192, 384), F32)],
        0,
        9,
    )(*parts, *labels, spread)
    from_right = neighbour(tile[0:2], "px", -1)
    from_left = neighbour(tile[34:36], "px", 1)
    core = tile[2:34]
    core = core + jnp.pad(from_left, ((0, 30), (0, 0), (0, 0))) + jnp.pad(from_right, ((30, 0), (0, 0), (0, 0)))
    from_above = neighbour(core[:, 0:2], "py", -1)
    from_below = neighbour(core[:, 18:20], "py", 1)
    density = (
        core[:, 2:18]
        + jnp.pad(from_below, ((0, 0), (0, 14), (0, 0)))
        + jnp.pad(from_above, ((0, 0), (14, 0), (0, 0)))
    )
    return displacement, density


def solution(mesh):
    return jax.shard_map(
        per_device,
        mesh=mesh,
        in_specs=(P("px", "py", None), P("px", "py", None, None), P("px", "py", None)),
        out_specs=(P(None, "px", "py", None), P("px", "py", None)),
        check_vma=False,
    )
```

```python
import functools
import math

import jax
import jax.numpy as jnp
import numpy as np
from jax import lax
from jax.experimental import pallas as pl
from jax.experimental.pallas import tpu as pltpu
from jax.sharding import PartitionSpec as P

SECOND_ORDER = 3.0 / 7.0
HIGHEST = lax.Precision.HIGHEST
F32 = jnp.float32
BF16 = jnp.bfloat16
N = 256
VLIM = 60 * 1024 * 1024


def cas_table(a, b):
    angle = (np.multiply.outer(a, b) % N) * (2.0 * math.pi / N)
    return np.cos(angle) + np.sin(angle)


def plane_rows():
    r = np.arange(512)
    xh, q, xl, i = r % 4, r // 4 % 2, r // 8 % 8, r // 64
    return 32 * i + 8 * xh + xl, q


def constants():
    n = np.arange(N)
    tz = cas_table(n, n).astype(np.float32)
    x, q = plane_rows()
    lxs = (cas_table(x, x) * (q[:, None] == q[None, :])).astype(np.float32)
    lap = -4.0 * np.sin(math.pi * n / N) ** 2
    return tz, lxs, lap[x][:, None].astype(np.float32), lap[None, :].astype(np.float32), lap.astype(np.float32)


def block_select():
    sel = np.zeros((640, 8, 128), np.float32)

    def cell(x, y):
        return x * 16 + y

    for bx in range(4):
        for by in range(2):
            g = bx * 2 + by
            for a in range(8):
                x = 8 * bx + a
                for c in range(8):
                    sel[cell(x, 8 * by + c), g, a * 8 + c] = 1.0
                sel[544 + x if by == 0 else cell(x, 7), g, 80 + a] = 1.0
                sel[cell(x, 8) if by == 0 else 576 + x, g, 88 + a] = 1.0
            for c in range(8):
                y = 8 * by + c
                sel[512 + y if bx == 0 else cell(8 * bx - 1, y), g, 64 + c] = 1.0
                sel[528 + y if bx == 3 else cell(8 * bx + 8, y), g, 72 + c] = 1.0
    return sel.reshape(640, 1024)


def spread_z():
    sel = np.zeros((12, 32, N), np.float32)
    for s in range(12):
        for b in range(32):
            sel[s, b, (8 * b + s - 2) % N] = 1.0
    return sel.reshape(384, N)


TZ, LXS, LAPX, LAPY, LAP = constants()
SELECT = block_select()
SPREAD = spread_z()


def lane_iota(shape):
    return lax.broadcasted_iota(jnp.int32, shape, len(shape) - 1)


def swap_groups(vals, width):
    count = len(vals)
    group = lane_iota(vals[0].shape) // width
    step = 1
    while step < count:
        low = (group & step) == 0
        new = list(vals)
        for k in range(count):
            if k & step:
                continue
            a, b = vals[k], vals[k + step]
            new[k] = jnp.where(low, a, pltpu.roll(b, step * width, 1))
            new[k + step] = jnp.where(low, pltpu.roll(a, 128 - step * width, 1), b)
        vals = new
        step *= 2
    return vals


def split3(x):
    a = x.astype(BF16)
    r = x - a.astype(F32)
    b = r.astype(BF16)
    c = (r - b.astype(F32)).astype(BF16)
    return a, b, c


def split2(x):
    a = x.astype(BF16)
    return a, (x - a.astype(F32)).astype(BF16)


def bdot(a, b):
    return jnp.dot(a, b, preferred_element_type=F32)


MESH = pl.DeviceIdType.MESH
STEPS = ((1, 0), (-1, 0), (0, 1), (0, -1), (1, 1), (1, -1), (-1, 1), (-1, -1))
hdot = functools.partial(jnp.dot, precision=HIGHEST, preferred_element_type=F32)


def shift_rows(p, before, after):
    up = jnp.concatenate([p[1:], after], axis=0)
    down = jnp.concatenate([before, p[:-1]], axis=0)
    return up, down


def spline_taps(t):
    t = jnp.clip(t, -1.0, 1.0)
    up = jnp.maximum(t, 0.0)
    dn = up - t
    p3 = up * up * up * (1.0 / 6.0)
    n3 = dn * dn * dn * (1.0 / 6.0)
    sq = t * t
    both = p3 + n3
    base = sq * 0.5 + (1.0 / 6.0) - both
    half = t * 0.5
    return n3, base - half - 2.0 * n3, (2.0 / 3.0) - sq + 3.0 * both, base + half - 2.0 * p3, p3


def whole_kernel(
    lz_ref, p_ref, tz_ref, lxs_ref, lapx_ref, lapy_ref, sel_ref, orow_ref, ocol_ref, wcol_ref, sp_ref,
    disp_ref, dens_ref,
    pp, pys, pyr, pcr, yl, dyz, src, a_out, a_in, m_ref, b_out, b_in, phi, fys, fyr, ft_ref,
    c_out, c_in, ct_ref, cp, wx_ref, wy_ref, wz_ref, t_ref, d_ref, g_ref, h_ref, tile, rxr, rys, ryr, rcr,
    hss, hsr, fss, fsr, rss, rsr, ass, asr, bss, bsr, css, csr,
):
    ix, iy = lax.axis_index("px"), lax.axis_index("py")
    me = ix * 16 + iy
    barrier = pltpu.get_barrier_semaphore()

    def greet(k, carry):
        peer = lax.rem(me + k, 128)
        pl.semaphore_signal(barrier, 1, device_id=(peer // 16, lax.rem(peer, 16)), device_id_type=MESH)
        return carry

    lax.fori_loop(1, 128, greet, 0)

    def near(k, source, dest, ssem, rsem):
        dx, dy = STEPS[k]
        where = (lax.rem(ix + dx + 8, 8), lax.rem(iy + dy + 16, 16))
        copy = pltpu.make_async_remote_copy(
            source, dest, ssem.at[k], rsem.at[k], device_id=where, device_id_type=MESH
        )
        copy.start()
        return copy

    def scatter(out, into, ssem, rsem):
        def send(k, carry):
            peer = lax.rem(me + k, 128)
            pltpu.make_async_remote_copy(
                out.at[peer], into.at[me], ssem, rsem,
                device_id=(peer // 16, lax.rem(peer, 16)), device_id_type=MESH,
            ).start()
            return carry

        lax.fori_loop(1, 128, send, 0)
        into[me] = out[me]

    def settle(out, into, sem):
        pltpu.make_async_copy(out.at[pl.ds(0, 127)], into.at[pl.ds(0, 127)], sem).wait()

    pp[1:33] = p_ref[...]
    pys[0] = p_ref[:, 15, :]
    pys[1] = p_ref[:, 0, :]
    pl.semaphore_wait(barrier, 127)
    copies = [
        near(0, p_ref.at[31], pp.at[0], hss, hsr),
        near(1, p_ref.at[0], pp.at[33], hss, hsr),
        near(2, pys.at[0], pyr.at[0], hss, hsr),
        near(3, pys.at[1], pyr.at[1], hss, hsr),
        near(4, p_ref.at[31, pl.ds(8, 8)], pcr.at[0], hss, hsr),
        near(5, p_ref.at[31, pl.ds(0, 8)], pcr.at[1], hss, hsr),
        near(6, p_ref.at[0, pl.ds(8, 8)], pcr.at[2], hss, hsr),
        near(7, p_ref.at[0, pl.ds(0, 8)], pcr.at[3], hss, hsr),
    ]
    for copy in copies:
        copy.wait()
    yl[0, 0:1] = pcr[0, 7:8]
    yl[0, 1:33] = pyr[0]
    yl[0, 33:34] = pcr[2, 7:8]
    yl[1, 0:1] = pcr[1, 0:1]
    yl[1, 1:33] = pyr[1]
    yl[1, 33:34] = pcr[3, 0:1]

    def slopes(x, carry):
        p = pp[x]
        up, down = shift_rows(p, yl[0, pl.ds(x, 1)], yl[1, pl.ds(x, 1)])
        dyz[0, x] = up - down
        dyz[1, x] = pltpu.roll(p, N - 1, 1) - pltpu.roll(p, 1, 1)
        dyz[2, x] = up + down - 2.0 * p
        return carry

    lax.fori_loop(0, 34, slopes, 0)

    def quadratic(x, carry):
        p = pp[x + 1]
        yy = dyz[2, x + 1]
        xx = pp[x + 2] - 2.0 * p + pp[x]
        zz = pltpu.roll(p, N - 1, 1) + pltpu.roll(p, 1, 1) - 2.0 * p
        xy = dyz[0, x + 2] - dyz[0, x]
        xz = dyz[1, x + 2] - dyz[1, x]
        dy = dyz[0, x + 1]
        yz = pltpu.roll(dy, N - 1, 1) - pltpu.roll(dy, 1, 1)
        src[x] = xx * (yy + zz) + yy * zz - (xy * xy + xz * xz + yz * yz) * 0.0625
        return carry

    lax.fori_loop(0, 32, quadratic, 0)
    for xh in range(4):
        part = src[8 * xh : 8 * xh + 8].reshape(128, N)
        r = lax.dot_general(
            tz_ref[...], part, (((1,), (1,)), ((), ())), precision=HIGHEST, preferred_element_type=F32
        )
        a_out[:, xh, :] = r[:128]
        a_out[:, 4 + xh, :] = r[128:]
    scatter(a_out, a_in, ass, asr)
    settle(a_out, a_in, asr)

    def gather_planes(n, carry):
        i, h = n // 2, lax.rem(n, 2)
        vals = swap_groups([a_in[n * 8 + j] for j in range(8)], 16)
        for xl in range(8):
            m_ref[h, pl.ds(pl.multiple_of(i * 64 + xl * 8, 8), 8), :] = vals[xl]
        return carry

    lax.fori_loop(0, 16, gather_planes, 0)
    b = hdot(lxs_ref[...], hdot(jnp.concatenate([m_ref[0], m_ref[1]], axis=1), tz_ref[...]))
    first = lax.broadcasted_iota(jnp.int32, (512, 1), 0) // 4 % 2 == 0
    column = lapx_ref[...] + jnp.where(first, lz_ref[0, 0], lz_ref[0, 1])
    eigen = column + lapy_ref[...]
    anchor = eigen == 0.0
    scale = SECOND_ORDER / (N * N * N)
    b = b * jnp.where(anchor, 0.0, scale / jnp.where(anchor, -1.0, eigen))
    b = hdot(hdot(lxs_ref[...], b), tz_ref[...])
    m_ref[0] = b[:, :128]
    m_ref[1] = b[:, 128:]

    def scatter_planes(n, carry):
        i, h = n // 2, lax.rem(n, 2)
        vals = swap_groups([m_ref[h, pl.ds(pl.multiple_of(i * 64 + xl * 8, 8), 8), :] for xl in range(8)], 16)
        for j in range(8):
            b_out[n * 8 + j] = vals[j]
        return carry

    lax.fori_loop(0, 16, scatter_planes, 0)
    scatter(b_out, b_in, bss, bsr)
    settle(b_out, b_in, bsr)
    for xh in range(4):
        a = jnp.concatenate([b_in[:, xh, :], b_in[:, 4 + xh, :]], axis=0)
        phi[8 * xh + 1 : 8 * xh + 9] = p_ref[8 * xh : 8 * xh + 8] + hdot(a.T, tz_ref[...]).reshape(8, 16, N)
    fys[0] = phi[1:33, 15, :]
    fys[1] = phi[1:33, 0, :]
    copies = [
        near(0, phi.at[32], phi.at[0], fss, fsr),
        near(1, phi.at[1], phi.at[33], fss, fsr),
        near(2, fys.at[0], fyr.at[0], fss, fsr),
        near(3, fys.at[1], fyr.at[1], fss, fsr),
    ]
    for m in range(4):
        ft_ref[m] = phi[8 * m + 1 : 8 * m + 9].reshape(128, N).T
    orow, ocol = orow_ref[...], ocol_ref[...]
    r_i = lax.broadcasted_iota(jnp.int32, (256, 256), 0)
    c_i = lax.broadcasted_iota(jnp.int32, (256, 256), 1)
    same = jnp.where((ocol == orow) & (r_i < c_i), 1, 0)
    slot = jnp.sum(same, axis=0, keepdims=True) * 128 + orow
    hot = (lax.broadcasted_iota(jnp.int32, (512, 256), 0) == slot).astype(F32).astype(BF16)
    for copy in copies:
        copy.wait()
    faces = jnp.concatenate([phi[0], phi[33], fyr[0], fyr[1], jnp.zeros((32, N), F32)], axis=0)
    ft_ref[4] = faces.T
    ordered = jnp.concatenate(
        [jnp.concatenate([ft_ref[m, pl.ds(e, 32, stride=8), :] for e in range(8)], axis=0) for m in range(5)],
        axis=1,
    )
    sel = sel_ref[...]
    a, b, c = split3(ordered)
    w = bdot(a, sel) + bdot(b, sel) + bdot(c, sel)

    def slab(e, turn):
        rows = w[32 * e : 32 * e + 32]
        if turn:
            rows = pltpu.roll(rows, turn, 0)
        return jnp.concatenate([rows[:, 128 * g : 128 * g + 128] for g in range(8)], axis=0)

    zfaces = (slab(7, 1), slab(0, 31))
    lanes = lane_iota((256, 128))
    for e in range(0, 8, 2):
        pair = []
        for k in (e, e + 1):
            v = slab(k, 0)
            face = pltpu.roll(zfaces[k // 4], 96 - 16 * (k % 4), 1)
            v = jnp.where((lanes >= 96) & (lanes < 112), face, v)
            if k == 0:
                v = jnp.where(lanes == 112, wcol_ref[...] + 1.0, v)
            pair.append(v)
        a, b, c = split3(jnp.concatenate(pair, axis=1))
        o = bdot(hot, a) + bdot(hot, b) + bdot(hot, c)
        for r in range(4):
            c_out[r, :, e, :] = o[128 * r : 128 * r + 128, :128]
            c_out[r, :, e + 1, :] = o[128 * r : 128 * r + 128, 128:]
    for r in range(4):
        scatter(c_out.at[r], c_in.at[r], css.at[r], csr.at[r])

    def displace(x, carry):
        f = phi[x + 1]
        up, down = shift_rows(f, fyr[0, pl.ds(x, 1)], fyr[1, pl.ds(x, 1)])
        disp_ref[0, x] = (phi[x] - phi[x + 2]) * 0.5
        disp_ref[1, x] = (down - up) * 0.5
        disp_ref[2, x] = (pltpu.roll(f, 1, 1) - pltpu.roll(f, N - 1, 1)) * 0.5
        return carry

    lax.fori_loop(0, 32, displace, 0)
    sub = lax.broadcasted_iota(jnp.int32, (8, 8, 128), 1)
    sub5 = lax.broadcasted_iota(jnp.int32, (8, 128), 0)

    for r in range(4):
        settle(c_out.at[r], c_in.at[r], csr.at[r])
        for e in range(8):
            ct_ref[e] = c_in[r, :, e, :].T
            cp[e + 1, 1:9] = ct_ref[e, 0:64].reshape(8, 8, 128)
            cp[e + 1, 0] = ct_ref[e, 64:72]
            cp[e + 1, 9] = ct_ref[e, 72:80]
            k = 1 + 2 * (e % 4)
            cp[9 * (e // 4), k : k + 2] = ct_ref[e, 96:112].reshape(2, 8, 128)

        def taps(e, carry):
            f = cp[e + 1, 1:9]
            ym = jnp.stack([jnp.broadcast_to(ct_ref[e, 80 + k : 81 + k], (8, 128)) for k in range(8)])
            yp = jnp.stack([jnp.broadcast_to(ct_ref[e, 88 + k : 89 + k], (8, 128)) for k in range(8)])
            ym = jnp.where(sub == 0, ym, pltpu.roll(f, 1, 1))
            yp = jnp.where(sub == 7, yp, pltpu.roll(f, 7, 1))
            triples = (
                (wx_ref, cp[e + 1, 0:8], cp[e + 1, 2:10]),
                (wy_ref, ym, yp),
                (wz_ref, cp[e, 1:9], cp[e + 2, 1:9]),
            )
            for ref, lo, hi in triples:
                for d, tap in enumerate(spline_taps((lo - hi) * 0.5)):
                    ref[d, e] = tap
            return carry

        lax.fori_loop(0, 8, taps, 0)
        t_ref[...] = jnp.zeros_like(t_ref)

        def step(n, carry):
            a, dx = n // 5, lax.rem(n, 5)
            u = a + dx
            acc = [None] * 12
            for e in range(8):
                q = wx_ref[dx, e, a][None] * wy_ref[:, e, a]
                for dz in range(5):
                    v = q * wz_ref[dz, e, a][None]
                    s = e + dz
                    acc[s] = v if acc[s] is None else acc[s] + v
                for s in [e] if e < 7 else range(7, 12):
                    t_ref[u, s] = t_ref[u, s] + acc[s]
            return carry

        lax.fori_loop(0, 40, step, 0)

        def fold(u, carry):
            for s in range(12):
                lo = t_ref[u, s, 0]
                hi = jnp.zeros((8, 128), F32)
                for dy in range(1, 5):
                    turned = pltpu.roll(t_ref[u, s, dy], dy, 0)
                    lo = lo + jnp.where(sub5 >= dy, turned, 0.0)
                    hi = hi + jnp.where(sub5 >= dy, 0.0, turned)
                d_ref[r, s, u, 0:8, :] = lo
                d_ref[r, s, u, 8:16, :] = hi
            return carry

        lax.fori_loop(0, 12, fold, 0)

    ids = lane_iota((128, 256)).astype(F32) + 1.0
    hot = jnp.concatenate(
        [(jnp.broadcast_to(c_in[r, :, 0, :][:, 112:113], (128, 256)) == ids).astype(F32).astype(BF16) for r in range(4)],
        axis=0,
    )

    def collect(s, carry):
        d = jnp.concatenate([d_ref[r, s].reshape(192, 128) for r in range(4)], axis=1)
        a, b = split2(d)
        g_ref[s] = bdot(a, hot) + bdot(b, hot)
        return carry

    lax.fori_loop(0, 12, collect, 0)
    for half in range(2):
        for k in range(3):
            vals = [g_ref[4 * k + m][:, 128 * half : 128 * half + 128] for m in range(4)]
            vals = swap_groups(vals, 32)
            for gl in range(4):
                h_ref[half * 4 + gl, :, 128 * k : 128 * k + 128] = vals[gl]
    tile[...] = jnp.zeros_like(tile)
    sp = sp_ref[...]
    for g in range(8):
        a, b = split2(h_ref[g])
        o = (bdot(a, sp) + bdot(b, sp)).reshape(12, 16, N)
        bx, by = g // 2, g % 2
        tile[8 * bx : 8 * bx + 12, 8 * by : 8 * by + 16, :] += o
    for k in range(2):
        rys[0, k] = tile[2:34, 18 + k, :]
        rys[1, k] = tile[2:34, k, :]
    copies = [
        near(0, tile.at[pl.ds(34, 2)], rxr.at[0], rss, rsr),
        near(1, tile.at[pl.ds(0, 2)], rxr.at[1], rss, rsr),
        near(2, rys.at[0], ryr.at[0], rss, rsr),
        near(3, rys.at[1], ryr.at[1], rss, rsr),
        near(4, tile.at[pl.ds(34, 2), pl.ds(16, 8)], rcr.at[0], rss, rsr),
        near(5, tile.at[pl.ds(34, 2), pl.ds(0, 8)], rcr.at[1], rss, rsr),
        near(6, tile.at[pl.ds(0, 2), pl.ds(16, 8)], rcr.at[2], rss, rsr),
        near(7, tile.at[pl.ds(0, 2), pl.ds(0, 8)], rcr.at[3], rss, rsr),
    ]
    dens_ref[...] = tile[2:34, 2:18, :]
    for copy in copies:
        copy.wait()
    dens_ref[0:2] += rxr[0, :, 2:18, :]
    dens_ref[30:32] += rxr[1, :, 2:18, :]
    for k in range(2):
        dens_ref[:, k, :] += ryr[0, k]
        dens_ref[:, 14 + k, :] += ryr[1, k]
    dens_ref[0:2, 0:2] += rcr[0, :, 2:4]
    dens_ref[0:2, 14:16] += rcr[1, :, 0:2]
    dens_ref[30:32, 0:2] += rcr[2, :, 2:4]
    dens_ref[30:32, 14:16] += rcr[3, :, 0:2]
    settle(a_out, a_in, ass)
    settle(b_out, b_in, bss)
    for r in range(4):
        settle(c_out.at[r], c_in.at[r], css.at[r])


def vm(*shape):
    return pltpu.VMEM(shape, F32)


def sds(*shape):
    return jax.ShapeDtypeStruct(shape, F32)


def per_device(potential, owner, window):
    index = lax.axis_index("px") * 16 + lax.axis_index("py")
    lap = jnp.asarray(LAP)
    lz = jnp.stack([lap[index], lap[index + 128]]).reshape(1, 2)
    dma = pltpu.SemaphoreType.DMA
    scratch = [
        vm(34, 16, N), vm(2, 32, N), vm(2, 32, N), vm(4, 8, N), vm(2, 40, N), vm(3, 34, 16, N), vm(32, 16, N),
        vm(128, 8, 128), vm(128, 8, 128), vm(2, 512, 128), vm(128, 8, 128), vm(128, 8, 128),
        vm(34, 16, N), vm(2, 32, N), vm(2, 32, N), vm(5, N, 128),
        vm(4, 128, 8, 128), vm(4, 128, 8, 128), vm(8, 128, 128), vm(10, 10, 8, 128),
        vm(5, 8, 8, 8, 128), vm(5, 8, 8, 8, 128), vm(5, 8, 8, 8, 128), vm(12, 12, 5, 8, 128),
        vm(4, 12, 12, 16, 128), vm(12, 192, N), vm(8, 192, 384), vm(36, 24, N),
        vm(2, 2, 24, N), vm(2, 2, 32, N), vm(2, 2, 32, N), vm(4, 2, 8, N),
        dma((8,)), dma((8,)), dma((4,)), dma((4,)), dma((8,)), dma((8,)),
        dma, dma, dma, dma, dma((4,)), dma((4,)),
    ]
    vmem = pl.BlockSpec(memory_space=pltpu.VMEM)
    return pl.pallas_call(
        whole_kernel,
        out_shape=[sds(3, 32, 16, N), sds(32, 16, N)],
        in_specs=[pl.BlockSpec(memory_space=pltpu.SMEM)] + [vmem] * 10,
        out_specs=[vmem, vmem],
        scratch_shapes=scratch,
        compiler_params=pltpu.CompilerParams(vmem_limit_bytes=VLIM, collective_id=0, has_side_effects=True),
    )(
        lz, potential, jnp.asarray(TZ), jnp.asarray(LXS), jnp.asarray(LAPX), jnp.asarray(LAPY),
        jnp.asarray(SELECT, BF16), owner.reshape(1, 256), owner.reshape(256, 1),
        window.reshape(256, 1).astype(F32), jnp.asarray(SPREAD, BF16),
    )


def solution(mesh):
    return jax.shard_map(
        per_device,
        mesh=mesh,
        in_specs=(P("px", "py", None), P("px", "py", None, None), P("px", "py", None)),
        out_specs=(P(None, "px", "py", None), P("px", "py", None)),
        check_vma=False,
    )
```

```python
import functools
import math

import jax
import jax.numpy as jnp
import numpy as np
from jax import lax
from jax.experimental import pallas as pl
from jax.experimental.pallas import tpu as pltpu
from jax.sharding import PartitionSpec as P

SECOND_ORDER = 3.0 / 7.0
HIGHEST = lax.Precision.HIGHEST
F32 = jnp.float32
BF16 = jnp.bfloat16
N = 256
VLIM = 60 * 1024 * 1024


def cas_table(a, b):
    angle = (np.multiply.outer(a, b) % N) * (2.0 * math.pi / N)
    return np.cos(angle) + np.sin(angle)


def constants():
    n = np.arange(N)
    r = np.arange(N)
    x = 32 * (r // 32) + 4 * (r % 8) + r // 8 % 4
    lap = -4.0 * np.sin(math.pi * n / N) ** 2
    tables = np.stack([cas_table(n, n), cas_table(x, x), lap[x][:, None] + lap[None, :]])
    return tables.astype(np.float32), lap.astype(np.float32)


def block_select():
    sel = np.zeros((256, 2, 128), np.float32)
    for by in range(2):
        for a in range(8):
            for c in range(8):
                sel[a * 16 + 8 * by + c, by, a * 8 + c] = 1.0
            sel[160 + a if by == 0 else a * 16 + 7, by, 80 + a] = 1.0
            sel[a * 16 + 8 if by == 0 else 168 + a, by, 88 + a] = 1.0
        for c in range(8):
            sel[128 + 8 * by + c, by, 64 + c] = 1.0
            sel[144 + 8 * by + c, by, 72 + c] = 1.0
    return sel.reshape(256, 256)


def spread_z():
    sel = np.zeros((12, 32, N), np.float32)
    for s in range(12):
        for b in range(32):
            sel[s, b, (8 * b + s - 2) % N] = 1.0
    return sel.reshape(384, N)


TABLES, LAP = constants()
SELECT = block_select()
SPREAD = spread_z()


def lane_iota(shape):
    return lax.broadcasted_iota(jnp.int32, shape, len(shape) - 1)


def swap_groups(vals, width):
    count = len(vals)
    group = lane_iota(vals[0].shape) // width
    step = 1
    while step < count:
        low = (group & step) == 0
        new = list(vals)
        for k in range(count):
            if k & step:
                continue
            a, b = vals[k], vals[k + step]
            new[k] = jnp.where(low, a, pltpu.roll(b, step * width, 1))
            new[k + step] = jnp.where(low, pltpu.roll(a, 128 - step * width, 1), b)
        vals = new
        step *= 2
    return vals


def split3(x):
    a = x.astype(BF16)
    r = x - a.astype(F32)
    b = r.astype(BF16)
    c = (r - b.astype(F32)).astype(BF16)
    return a, b, c


def split2(x):
    a = x.astype(BF16)
    return a, (x - a.astype(F32)).astype(BF16)


def bdot(a, b):
    return jnp.dot(a, b, preferred_element_type=F32)


MESH = pl.DeviceIdType.MESH
STEPS = ((1, 0), (-1, 0), (0, 1), (0, -1), (1, 1), (1, -1), (-1, 1), (-1, -1))
hdot = functools.partial(jnp.dot, precision=HIGHEST, preferred_element_type=F32)


def dot3(a, b):
    return bdot(a[0], b[0]) + (bdot(a[0], b[1]) + bdot(a[1], b[0]))


def rows_dot3(a, b):
    def one(x, y):
        return lax.dot_general(x, y, (((1,), (1,)), ((), ())), preferred_element_type=F32)

    return one(a[0], b[0]) + (one(a[0], b[1]) + one(a[1], b[0]))


def pair_halves(a, b):
    low = lane_iota(a.shape) < 64
    return jnp.where(low, a, pltpu.roll(b, 64, 1)), jnp.where(low, pltpu.roll(a, 64, 1), b)


def shift_rows(p, before, after):
    up = jnp.concatenate([p[1:], after], axis=0)
    down = jnp.concatenate([before, p[:-1]], axis=0)
    return up, down


def spline_taps(t):
    t = jnp.clip(t, -1.0, 1.0)
    up = jnp.maximum(t, 0.0)
    dn = up - t
    p3 = up * up * up * (1.0 / 6.0)
    n3 = dn * dn * dn * (1.0 / 6.0)
    sq = t * t
    both = p3 + n3
    base = sq * 0.5 + (1.0 / 6.0) - both
    half = t * 0.5
    return n3, base - half - 2.0 * n3, (2.0 / 3.0) - sq + 3.0 * both, base + half - 2.0 * p3, p3


def whole_kernel(
    lap_ref, orow_ref, wrow_ref, p_hbm, tab_hbm, sel_hbm, sp_hbm,
    phi, fyr, dens_ref,
    pp, tab, sel_ref, sp_ref, tz, lx, hot_ref, wcol,
    ft_all, w_ref, pys, pyr, pcr, yl, src, a_out, a_in, m_ref, b_out, b_in, fys,
    c_out, c_in, ct_ref, cp, wx_ref, wy_ref, wz_ref, d_ref, g_ref, h_ref, tile, rxr, rys, ryr, rcr,
    lsem, hss, hsr, fss, fsr, rss, rsr, ass, asr, bss, bsr, css, csr,
):
    ix, iy = lax.axis_index("px"), lax.axis_index("py")
    me = ix * 16 + iy
    barrier = pltpu.get_barrier_semaphore()

    cx, core, cy, cz = ix // 2, lax.rem(ix, 2), iy // 4, lax.rem(iy, 4)

    def each_peer(act):
        def group(n, skip):
            side = lax.rem(core + lax.rem(n, 2), 2)
            for b in range(4):
                for d in range(4):
                    if skip and b == 3 and d == 3:
                        continue
                    px = lax.rem(cx + n // 2 + b + d + 2, 4) * 2 + side
                    py = lax.rem(cy + b + 1, 4) * 4 + lax.rem(cz + d + 1, 4)
                    act(px, py)

        def later(n, carry):
            group(n, False)
            return carry

        group(0, True)
        lax.fori_loop(1, 8, later, 0)

    def greet(px, py):
        pl.semaphore_signal(barrier, 1, device_id=(px, py), device_id_type=MESH)

    each_peer(greet)

    def near(k, source, dest, ssem, rsem):
        dx, dy = STEPS[k]
        where = (lax.rem(ix + dx + 8, 8), lax.rem(iy + dy + 16, 16))
        copy = pltpu.make_async_remote_copy(
            source, dest, ssem.at[k], rsem.at[k], device_id=where, device_id_type=MESH
        )
        copy.start()
        return copy

    def scatter(out, into, ssem, rsem):
        def send(px, py):
            pltpu.make_async_remote_copy(
                out.at[px * 16 + py], into.at[me], ssem, rsem, device_id=(px, py), device_id_type=MESH
            ).start()

        each_peer(send)
        into[me] = out[me]

    def settle(out, into, sem):
        pltpu.make_async_copy(out.at[pl.ds(0, 127)], into.at[pl.ds(0, 127)], sem).wait()

    loads = [
        pltpu.make_async_copy(p_hbm, pp.at[pl.ds(1, 32)], lsem.at[0]),
        pltpu.make_async_copy(tab_hbm, tab, lsem.at[1]),
        pltpu.make_async_copy(sel_hbm, sel_ref, lsem.at[2]),
        pltpu.make_async_copy(sp_hbm, sp_ref, lsem.at[3]),
    ]
    for load in loads:
        load.start()
    wide = jnp.broadcast_to(orow_ref[...].astype(F32), (256, 256))
    r_i = lax.broadcasted_iota(jnp.int32, (256, 256), 0)
    c_i = lax.broadcasted_iota(jnp.int32, (256, 256), 1)
    same = jnp.where((wide.T == wide) & (r_i < c_i), 1, 0)
    slot = jnp.sum(same, axis=0, keepdims=True) * 128 + orow_ref[...]
    hot_ref[...] = (lax.broadcasted_iota(jnp.int32, (512, 256), 0) == slot).astype(F32).astype(BF16)
    wcol[...] = jnp.broadcast_to(wrow_ref[...].astype(F32) + 1.0, (128, 256)).T
    loads[0].wait()
    pys[0] = pp[1:33, 15, :]
    pys[1] = pp[1:33, 0, :]
    loads[1].wait()
    tz[0], tz[1] = split2(tab[0])
    lx[0], lx[1] = split2(tab[1])
    pl.semaphore_wait(barrier, 127)
    copies = [
        near(0, pp.at[32], pp.at[0], hss, hsr),
        near(1, pp.at[1], pp.at[33], hss, hsr),
        near(2, pys.at[0], pyr.at[0], hss, hsr),
        near(3, pys.at[1], pyr.at[1], hss, hsr),
        near(4, pp.at[32, pl.ds(8, 8)], pcr.at[0], hss, hsr),
        near(5, pp.at[32, pl.ds(0, 8)], pcr.at[1], hss, hsr),
        near(6, pp.at[1, pl.ds(8, 8)], pcr.at[2], hss, hsr),
        near(7, pp.at[1, pl.ds(0, 8)], pcr.at[3], hss, hsr),
    ]
    for copy in copies:
        copy.wait()
    yl[0, 0:1] = pcr[0, 7:8]
    yl[0, 1:33] = pyr[0]
    yl[0, 33:34] = pcr[2, 7:8]
    yl[1, 0:1] = pcr[1, 0:1]
    yl[1, 1:33] = pyr[1]
    yl[1, 33:34] = pcr[3, 0:1]

    planes = []
    for x in range(34):
        p = pp[x]
        up, down = shift_rows(p, yl[0, x : x + 1], yl[1, x : x + 1])
        ahead, behind = pltpu.roll(p, N - 1, 1), pltpu.roll(p, 1, 1)
        planes.append((p, up - down, ahead - behind, up + down - 2.0 * p, ahead + behind - 2.0 * p))
        if x < 2:
            continue
        (p0, dy0, dz0, _, _), (p1, dy1, _, yy, zz), (p2, dy2, dz2, _, _) = planes[-3:]
        xx = p2 - 2.0 * p1 + p0
        xy, xz = dy2 - dy0, dz2 - dz0
        yz = pltpu.roll(dy1, N - 1, 1) - pltpu.roll(dy1, 1, 1)
        src[x - 2] = xx * (yy + zz) + yy * zz - (xy * xy + xz * xz + yz * yz) * 0.0625
        if x % 8 == 1:
            h = x // 8 - 1
            part = split2(src[8 * h : 8 * h + 8].reshape(128, N))
            r = rows_dot3((tz[0], tz[1]), part)
            a_out[:, 2 * h, :], a_out[:, 2 * h + 1, :] = pair_halves(r[:128], r[128:])
    scatter(a_out, a_in, ass, asr)
    settle(a_out, a_in, asr)

    for i in range(8):
        for h in range(2):
            vals = swap_groups([a_in[i * 16 + h * 8 + k] for k in range(8)], 16)
            for k in range(8):
                row = (k // 4) * 256 + i * 32 + (k % 4) * 8
                m_ref[row : row + 8, 128 * h : 128 * h + 128] = vals[k]
    tzs, lxs = (tz[0], tz[1]), (lx[0], lx[1])
    b = dot3(split2(m_ref[...]), tzs)
    scale = SECOND_ORDER / (N * N * N)
    halves = []
    for q in range(2):
        c = dot3(lxs, split2(b[256 * q : 256 * q + 256]))
        eigen = tab[2] + lap_ref[me + 128 * q]
        anchor = eigen == 0.0
        c = c * jnp.where(anchor, 0.0, scale / jnp.where(anchor, -1.0, eigen))
        halves.append(hdot(tab[1], c))
    m_ref[...] = hdot(jnp.concatenate(halves, axis=0), tab[0])
    for i in range(8):
        for h in range(2):
            vals = []
            for k in range(8):
                row = (k // 4) * 256 + i * 32 + (k % 4) * 8
                vals.append(m_ref[row : row + 8, 128 * h : 128 * h + 128])
            vals = swap_groups(vals, 16)
            for k in range(8):
                b_out[i * 16 + h * 8 + k] = vals[k]
    scatter(b_out, b_in, bss, bsr)
    settle(b_out, b_in, bsr)
    for h in range(4):
        a = jnp.concatenate(pair_halves(b_in[:, 2 * h, :], b_in[:, 2 * h + 1, :]), axis=0)
        phi[8 * h + 1 : 8 * h + 9] = pp[8 * h + 1 : 8 * h + 9] + hdot(a.T, tab[0]).reshape(8, 16, N)
    fys[0] = phi[1:33, 15, :]
    fys[1] = phi[1:33, 0, :]
    copies = [
        near(0, phi.at[32], phi.at[0], fss, fsr),
        near(1, phi.at[1], phi.at[33], fss, fsr),
        near(2, fys.at[0], fyr.at[0], fss, fsr),
        near(3, fys.at[1], fyr.at[1], fss, fsr),
    ]
    loads[2].wait()
    loads[3].wait()

    def chosen(ft, sel):
        out = 0.0
        for part in split3(jnp.concatenate([ft[pl.ds(e, 32, stride=8), :] for e in range(8)], axis=0)):
            out = out + bdot(part, sel)
        return out

    for m in range(4):
        ft_all[m] = phi[8 * m + 1 : 8 * m + 9].reshape(128, N).T
        w_ref[:, 256 * m : 256 * m + 256] = chosen(ft_all.at[m], sel_ref[0:128])
    for copy in copies:
        copy.wait()
    w = []
    for m in range(4):
        faces = jnp.concatenate(
            [phi[8 * m], phi[8 * m + 9], fyr[0, 8 * m : 8 * m + 8], fyr[1, 8 * m : 8 * m + 8], jnp.zeros((80, N), F32)],
            axis=0,
        )
        ft_all[m] = faces.T
        w.append(w_ref[:, 256 * m : 256 * m + 256] + chosen(ft_all.at[m], sel_ref[128:256]))
    w = jnp.concatenate(w, axis=1)

    def slab(e, turn):
        rows = w[32 * e : 32 * e + 32]
        if turn:
            rows = pltpu.roll(rows, turn, 0)
        return jnp.concatenate([rows[:, 128 * g : 128 * g + 128] for g in range(8)], axis=0)

    zfaces = (slab(7, 1), slab(0, 31))
    lanes = lane_iota((256, 128))
    hot = hot_ref[...]
    for e in range(0, 8, 2):
        pair = []
        for k in (e, e + 1):
            v = slab(k, 0)
            face = pltpu.roll(zfaces[k // 4], 96 - 16 * (k % 4), 1)
            v = jnp.where((lanes >= 96) & (lanes < 112), face, v)
            if k == 0:
                v = jnp.where(lanes == 112, wcol[...], v)
            pair.append(v)
        a, b, c = split3(jnp.concatenate(pair, axis=1))
        o = bdot(hot, a) + bdot(hot, b) + bdot(hot, c)
        for r in range(4):
            c_out[r, :, e, :] = o[128 * r : 128 * r + 128, :128]
            c_out[r, :, e + 1, :] = o[128 * r : 128 * r + 128, 128:]
    for r in range(2):
        scatter(c_out.at[r], c_in.at[r], css.at[r], csr.at[r])

    sub = lax.broadcasted_iota(jnp.int32, (8, 8, 128), 1)
    sub5 = lax.broadcasted_iota(jnp.int32, (8, 128), 0)
    ids = lane_iota((128, 256)).astype(F32) + 1.0

    for r in range(4):
        settle(c_out.at[r], c_in.at[r], csr.at[r])
        if r < 2:
            scatter(c_out.at[r + 2], c_in.at[r + 2], css.at[r + 2], csr.at[r + 2])
        for e in range(8):
            ct_ref[e] = c_in[r, :, e, :].T
            cp[e + 1, 1:9] = ct_ref[e, 0:64].reshape(8, 8, 128)
            cp[e + 1, 0] = ct_ref[e, 64:72]
            cp[e + 1, 9] = ct_ref[e, 72:80]
            k = 1 + 2 * (e % 4)
            cp[9 * (e // 4), k : k + 2] = ct_ref[e, 96:112].reshape(2, 8, 128)

        def taps(e, carry):
            f = cp[e + 1, 1:9]
            ym = jnp.stack([jnp.broadcast_to(ct_ref[e, 80 + k : 81 + k], (8, 128)) for k in range(8)])
            yp = jnp.stack([jnp.broadcast_to(ct_ref[e, 88 + k : 89 + k], (8, 128)) for k in range(8)])
            ym = jnp.where(sub == 0, ym, pltpu.roll(f, 1, 1))
            yp = jnp.where(sub == 7, yp, pltpu.roll(f, 7, 1))
            triples = (
                (wx_ref, cp[e + 1, 0:8], cp[e + 1, 2:10]),
                (wy_ref, ym, yp),
                (wz_ref, cp[e, 1:9], cp[e + 2, 1:9]),
            )
            for ref, lo, hi in triples:
                for d, tap in enumerate(spline_taps((lo - hi) * 0.5)):
                    ref[d, e] = tap
            return carry

        lax.fori_loop(0, 8, taps, 0)
        for u in range(12):
            acc = [None] * 12
            for e in range(8):
                for a in range(max(0, u - 4), min(8, u + 1)):
                    q = wx_ref[u - a, e, a][None] * wy_ref[:, e, a]
                    for dz in range(5):
                        v = q * wz_ref[dz, e, a][None]
                        k = e + dz
                        acc[k] = v if acc[k] is None else acc[k] + v
                for k in [e] if e < 7 else range(7, 12):
                    turned = [pltpu.roll(acc[k][dy], dy, 0) for dy in range(1, 5)]
                    over = [jnp.where(sub5 < dy, t, 0.0) for dy, t in enumerate(turned, 1)]
                    hi = (over[0] + over[1]) + (over[2] + over[3])
                    d_ref[k, r % 2, u, 0:8, :] = acc[k][0] + (turned[0] + turned[1]) + (turned[2] + turned[3]) - hi
                    d_ref[k, r % 2, u, 8:16, :] = hi

        if r % 2 == 1:
            hot2 = jnp.concatenate(
                [
                    (jnp.broadcast_to(c_in[k, :, 0, :][:, 112:113], (128, 256)) == ids).astype(F32).astype(BF16)
                    for k in (r - 1, r)
                ],
                axis=0,
            )
            for s in range(12):
                d = jnp.concatenate([d_ref[s, k].reshape(192, 128) for k in range(2)], axis=1)
                a, b = split2(d)
                o = bdot(a, hot2) + bdot(b, hot2)
                g_ref[s] = o if r == 1 else g_ref[s] + o

    for half in range(2):
        for k in range(3):
            vals = [g_ref[4 * k + m][:, 128 * half : 128 * half + 128] for m in range(4)]
            vals = swap_groups(vals, 32)
            for gl in range(4):
                h_ref[half * 4 + gl, :, 128 * k : 128 * k + 128] = vals[gl]
    tile[...] = jnp.zeros_like(tile)
    sp = sp_ref[...]
    for g in range(8):
        a, b = split2(h_ref[g])
        o = (bdot(a, sp) + bdot(b, sp)).reshape(12, 16, N)
        bx, by = g // 2, g % 2
        tile[8 * bx : 8 * bx + 12, 8 * by : 8 * by + 16, :] += o
    for k in range(2):
        rys[0, k] = tile[2:34, 18 + k, :]
        rys[1, k] = tile[2:34, k, :]
    copies = [
        near(0, tile.at[pl.ds(34, 2)], rxr.at[0], rss, rsr),
        near(1, tile.at[pl.ds(0, 2)], rxr.at[1], rss, rsr),
        near(2, rys.at[0], ryr.at[0], rss, rsr),
        near(3, rys.at[1], ryr.at[1], rss, rsr),
        near(4, tile.at[pl.ds(34, 2), pl.ds(16, 8)], rcr.at[0], rss, rsr),
        near(5, tile.at[pl.ds(34, 2), pl.ds(0, 8)], rcr.at[1], rss, rsr),
        near(6, tile.at[pl.ds(0, 2), pl.ds(16, 8)], rcr.at[2], rss, rsr),
        near(7, tile.at[pl.ds(0, 2), pl.ds(0, 8)], rcr.at[3], rss, rsr),
    ]
    dens_ref[...] = tile[2:34, 2:18, :]
    for copy in copies:
        copy.wait()
    dens_ref[0:2] += rxr[0, :, 2:18, :]
    dens_ref[30:32] += rxr[1, :, 2:18, :]
    for k in range(2):
        dens_ref[:, k, :] += ryr[0, k]
        dens_ref[:, 14 + k, :] += ryr[1, k]
    dens_ref[0:2, 0:2] += rcr[0, :, 2:4]
    dens_ref[0:2, 14:16] += rcr[1, :, 0:2]
    dens_ref[30:32, 0:2] += rcr[2, :, 2:4]
    dens_ref[30:32, 14:16] += rcr[3, :, 0:2]
    settle(a_out, a_in, ass)
    settle(b_out, b_in, bss)
    for r in range(4):
        settle(c_out.at[r], c_in.at[r], css.at[r])


def finish_kernel(phi, fyr, dens, disp_ref, out_ref, buf, sem):
    copies = [pltpu.make_async_copy(dens, out_ref, sem.at[4])]
    copies[0].start()
    for g in range(4):
        for x in range(8 * g, 8 * g + 8):
            f = phi[x + 1]
            up, down = shift_rows(f, fyr[0, x : x + 1], fyr[1, x : x + 1])
            buf[0, x] = (phi[x] - phi[x + 2]) * 0.5
            buf[1, x] = (down - up) * 0.5
            buf[2, x] = (pltpu.roll(f, 1, 1) - pltpu.roll(f, N - 1, 1)) * 0.5
        part = pl.ds(8 * g, 8)
        copies.append(pltpu.make_async_copy(buf.at[:, part], disp_ref.at[:, part], sem.at[g]))
        copies[-1].start()
    for copy in copies:
        copy.wait()


def vm(*shape):
    return pltpu.VMEM(shape, F32)


def sds(*shape):
    return jax.ShapeDtypeStruct(shape, F32)


def per_device(potential, owner, window):
    dma = pltpu.SemaphoreType.DMA
    scratch = [
        vm(34, 16, N), vm(3, N, N), pltpu.VMEM((N, N), BF16), pltpu.VMEM((384, N), BF16),
        pltpu.VMEM((2, N, N), BF16), pltpu.VMEM((2, N, N), BF16), pltpu.VMEM((512, N), BF16), vm(N, 128),
        vm(4, N, 128), vm(N, 1024), vm(2, 32, N), vm(2, 32, N), vm(4, 8, N), vm(2, 40, N), vm(32, 16, N),
        vm(128, 8, 128), vm(128, 8, 128), vm(512, N), vm(128, 8, 128), vm(128, 8, 128), vm(2, 32, N),
        vm(4, 128, 8, 128), vm(4, 128, 8, 128), vm(8, 128, 128), vm(10, 10, 8, 128),
        vm(5, 8, 8, 8, 128), vm(5, 8, 8, 8, 128), vm(5, 8, 8, 8, 128),
        vm(12, 2, 12, 16, 128), vm(12, 192, N), vm(8, 192, 384), vm(36, 24, N),
        vm(2, 2, 24, N), vm(2, 2, 32, N), vm(2, 2, 32, N), vm(4, 2, 8, N),
        dma((4,)), dma((8,)), dma((8,)), dma((4,)), dma((4,)), dma((8,)), dma((8,)),
        dma, dma, dma, dma, dma((4,)), dma((4,)),
    ]
    vmem = pl.BlockSpec(memory_space=pltpu.VMEM)
    hbm = pl.BlockSpec(memory_space=pl.ANY)
    phi, sides, dens = pl.pallas_call(
        whole_kernel,
        out_shape=[sds(34, 16, N), sds(2, 32, N), sds(32, 16, N)],
        in_specs=[pl.BlockSpec(memory_space=pltpu.SMEM), vmem, vmem, hbm, hbm, hbm, hbm],
        out_specs=[vmem, vmem, vmem],
        scratch_shapes=scratch,
        compiler_params=pltpu.CompilerParams(vmem_limit_bytes=VLIM, collective_id=0, has_side_effects=True),
    )(
        jnp.asarray(LAP), owner.reshape(1, 256), window.reshape(1, 256), potential, jnp.asarray(TABLES),
        jnp.asarray(SELECT, BF16), jnp.asarray(SPREAD, BF16),
    )
    return pl.pallas_call(
        finish_kernel,
        out_shape=[sds(3, 32, 16, N), sds(32, 16, N)],
        in_specs=[vmem, vmem, vmem],
        out_specs=[hbm, hbm],
        scratch_shapes=[vm(3, 32, 16, N), dma((5,))],
        compiler_params=pltpu.CompilerParams(vmem_limit_bytes=VLIM),
    )(phi, sides, dens)


def solution(mesh):
    return jax.shard_map(
        per_device,
        mesh=mesh,
        in_specs=(P("px", "py", None), P("px", "py", None, None), P("px", "py", None)),
        out_specs=(P(None, "px", "py", None), P("px", "py", None)),
        check_vma=False,
    )
```

```python
import functools
import math

import jax
import jax.numpy as jnp
import numpy as np
from jax import lax
from jax.experimental import pallas as pl
from jax.experimental.pallas import tpu as pltpu
from jax.sharding import PartitionSpec as P

SECOND_ORDER = 3.0 / 7.0
HIGHEST = lax.Precision.HIGHEST
F32 = jnp.float32
BF16 = jnp.bfloat16
N = 256
VLIM = 60 * 1024 * 1024


def cas_table(a, b):
    angle = (np.multiply.outer(a, b) % N) * (2.0 * math.pi / N)
    return np.cos(angle) + np.sin(angle)


def constants():
    n = np.arange(N)
    r = np.arange(N)
    x = 32 * (r // 32) + 4 * (r % 8) + r // 8 % 4
    lap = -4.0 * np.sin(math.pi * n / N) ** 2
    tables = np.stack([cas_table(n, n), cas_table(x, x), lap[x][:, None] + lap[None, :]])
    return tables.astype(np.float32), lap.astype(np.float32)


def block_select():
    sel = np.zeros((256, 2, 128), np.float32)
    for by in range(2):
        for a in range(8):
            for c in range(8):
                sel[a * 16 + 8 * by + c, by, a * 8 + c] = 1.0
            sel[160 + a if by == 0 else a * 16 + 7, by, 80 + a] = 1.0
            sel[a * 16 + 8 if by == 0 else 168 + a, by, 88 + a] = 1.0
        for c in range(8):
            sel[128 + 8 * by + c, by, 64 + c] = 1.0
            sel[144 + 8 * by + c, by, 72 + c] = 1.0
    return sel.reshape(256, 256)


def spread_z():
    sel = np.zeros((12, 32, N), np.float32)
    for s in range(12):
        for b in range(32):
            sel[s, b, (8 * b + s - 2) % N] = 1.0
    return sel.reshape(384, N)


TABLES, LAP = constants()
SELECT = block_select()
SPREAD = spread_z()


def lane_iota(shape):
    return lax.broadcasted_iota(jnp.int32, shape, len(shape) - 1)


def swap_groups(vals, width):
    count = len(vals)
    group = lane_iota(vals[0].shape) // width
    turned = [pltpu.roll(v, k * width, 1) if k else v for k, v in enumerate(vals)]
    step = 1
    while step < count:
        high = (group & step) != 0
        turned = [jnp.where(high, turned[(k + step) % count], turned[k]) for k in range(count)]
        step *= 2
    return [pltpu.roll(turned[-k % count], 128 - k * width, 1) if k else turned[0] for k in range(count)]


def split3(x):
    a = x.astype(BF16)
    r = x - a.astype(F32)
    b = r.astype(BF16)
    c = (r - b.astype(F32)).astype(BF16)
    return a, b, c


def split2(x):
    a = x.astype(BF16)
    return a, (x - a.astype(F32)).astype(BF16)


def bdot(a, b):
    return jnp.dot(a, b, preferred_element_type=F32)


MESH = pl.DeviceIdType.MESH


def torus_rings():
    rings = [[] for _ in range(7)]
    for a in range(4):
        for b in range(4):
            for d in range(4):
                rings[sum(min(o, 4 - o) for o in (a, b, d))].append((a, b, d))
    return rings[::-1]


RINGS = torus_rings()
STEPS = ((1, 0), (-1, 0), (0, 1), (0, -1), (1, 1), (1, -1), (-1, 1), (-1, -1))
hdot = functools.partial(jnp.dot, precision=HIGHEST, preferred_element_type=F32)


def dot3(a, b):
    return bdot(a[0], b[0]) + (bdot(a[0], b[1]) + bdot(a[1], b[0]))


def rows_dot3(a, b):
    def one(x, y):
        return lax.dot_general(x, y, (((1,), (1,)), ((), ())), preferred_element_type=F32)

    return one(a[0], b[0]) + (one(a[0], b[1]) + one(a[1], b[0]))


def pair_halves(a, b):
    low = lane_iota(a.shape) < 64
    return jnp.where(low, a, pltpu.roll(b, 64, 1)), jnp.where(low, pltpu.roll(a, 64, 1), b)


def shift_rows(p, before, after):
    up = jnp.concatenate([p[1:], after], axis=0)
    down = jnp.concatenate([before, p[:-1]], axis=0)
    return up, down


def spline_taps(t):
    t = jnp.clip(t, -1.0, 1.0)
    up = jnp.maximum(t, 0.0)
    dn = up - t
    p3 = up * up * up * (1.0 / 6.0)
    n3 = dn * dn * dn * (1.0 / 6.0)
    sq = t * t
    both = p3 + n3
    base = sq * 0.5 + (1.0 / 6.0) - both
    half = t * 0.5
    return n3, base - half - 2.0 * n3, (2.0 / 3.0) - sq + 3.0 * both, base + half - 2.0 * p3, p3


def whole_kernel(
    lap_ref, orow_ref, wrow_ref, p_hbm, tab_hbm, sel_hbm, sp_hbm,
    phi, fyr, dens_ref,
    pp, tab, sel_ref, sp_ref, tz, lx, hot_ref, wcol,
    ft_all, w_ref, pys, pyr, pcr, yl, src, a_out, a_in, m_ref, b_out, b_in, fys,
    c_out, c_in, l_out, l_in, named_ref, ct_ref, cp, wx_ref, wy_ref, wz_ref, d_ref, g_ref, h_ref, tile, rxr, rys, ryr, rcr,
    lsem, hss, hsr, fss, fsr, rss, rsr, ass, asr, bss, bsr, css, csr, qss, qsr,
):
    ix, iy = lax.axis_index("px"), lax.axis_index("py")
    me = ix * 16 + iy
    barrier = pltpu.get_barrier_semaphore()

    cx, core, cy, cz = ix // 2, lax.rem(ix, 2), iy // 4, lax.rem(iy, 4)

    def each_peer(act):
        for offsets in RINGS:

            def ring(n, carry, offsets=offsets):
                side = lax.rem(core + n + 1, 2)
                for a, b, d in offsets:
                    act(lax.rem(cx + a, 4) * 2 + side, lax.rem(cy + b, 4) * 4 + lax.rem(cz + d, 4))
                return carry

            lax.fori_loop(0, 2 if offsets[0] != (0, 0, 0) else 1, ring, 0)

    def greet(px, py):
        pl.semaphore_signal(barrier, 1, device_id=(px, py), device_id_type=MESH)

    each_peer(greet)

    def near(k, source, dest, ssem, rsem):
        dx, dy = STEPS[k]
        where = (lax.rem(ix + dx + 8, 8), lax.rem(iy + dy + 16, 16))
        copy = pltpu.make_async_remote_copy(
            source, dest, ssem.at[k], rsem.at[k], device_id=where, device_id_type=MESH
        )
        copy.start()
        return copy

    def scatter(out, into, ssem, rsem):
        def send(px, py):
            pltpu.make_async_remote_copy(
                out.at[px * 16 + py], into.at[me], ssem, rsem, device_id=(px, py), device_id_type=MESH
            ).start()

        each_peer(send)
        into[me] = out[me]

    def settle(out, into, sem):
        pltpu.make_async_copy(out.at[pl.ds(0, 127)], into.at[pl.ds(0, 127)], sem).wait()

    loads = [
        pltpu.make_async_copy(p_hbm, pp.at[pl.ds(1, 32)], lsem.at[0]),
        pltpu.make_async_copy(tab_hbm, tab, lsem.at[1]),
        pltpu.make_async_copy(sel_hbm, sel_ref, lsem.at[2]),
        pltpu.make_async_copy(sp_hbm, sp_ref, lsem.at[3]),
    ]
    for load in loads:
        load.start()
    wide = jnp.broadcast_to(orow_ref[...].astype(F32), (256, 256))
    r_i = lax.broadcasted_iota(jnp.int32, (256, 256), 0)
    c_i = lax.broadcasted_iota(jnp.int32, (256, 256), 1)
    same = jnp.where((wide.T == wide) & (r_i < c_i), 1, 0)
    slot = jnp.sum(same, axis=0, keepdims=True) * 128 + orow_ref[...]
    hot_ref[...] = (lax.broadcasted_iota(jnp.int32, (512, 256), 0) == slot).astype(F32).astype(BF16)
    wcol[...] = jnp.broadcast_to(wrow_ref[...].astype(F32) + 1.0, (128, 256)).T
    loads[0].wait()
    pys[0] = pp[1:33, 15, :]
    pys[1] = pp[1:33, 0, :]
    loads[1].wait()
    tz[0], tz[1] = split2(tab[0])
    lx[0], lx[1] = split2(tab[1])
    pl.semaphore_wait(barrier, 127)
    copies = [
        near(0, pp.at[32], pp.at[0], hss, hsr),
        near(1, pp.at[1], pp.at[33], hss, hsr),
        near(2, pys.at[0], pyr.at[0], hss, hsr),
        near(3, pys.at[1], pyr.at[1], hss, hsr),
        near(4, pp.at[32, pl.ds(8, 8)], pcr.at[0], hss, hsr),
        near(5, pp.at[32, pl.ds(0, 8)], pcr.at[1], hss, hsr),
        near(6, pp.at[1, pl.ds(8, 8)], pcr.at[2], hss, hsr),
        near(7, pp.at[1, pl.ds(0, 8)], pcr.at[3], hss, hsr),
    ]
    for copy in copies:
        copy.wait()
    yl[0, 0:1] = pcr[0, 7:8]
    yl[0, 1:33] = pyr[0]
    yl[0, 33:34] = pcr[2, 7:8]
    yl[1, 0:1] = pcr[1, 0:1]
    yl[1, 1:33] = pyr[1]
    yl[1, 33:34] = pcr[3, 0:1]

    planes = []
    for x in range(34):
        p = pp[x]
        up, down = shift_rows(p, yl[0, x : x + 1], yl[1, x : x + 1])
        ahead, behind = pltpu.roll(p, N - 1, 1), pltpu.roll(p, 1, 1)
        planes.append((p, up - down, ahead - behind, up + down - 2.0 * p, ahead + behind - 2.0 * p))
        if x < 2:
            continue
        (p0, dy0, dz0, _, _), (p1, dy1, _, yy, zz), (p2, dy2, dz2, _, _) = planes[-3:]
        xx = p2 - 2.0 * p1 + p0
        xy, xz = dy2 - dy0, dz2 - dz0
        yz = pltpu.roll(dy1, N - 1, 1) - pltpu.roll(dy1, 1, 1)
        src[x - 2] = xx * (yy + zz) + yy * zz - (xy * xy + xz * xz + yz * yz) * 0.0625
        if x % 8 == 1:
            h = x // 8 - 1
            part = split2(src[8 * h : 8 * h + 8].reshape(128, N))
            r = rows_dot3((tz[0], tz[1]), part)
            a_out[:, 2 * h, :], a_out[:, 2 * h + 1, :] = pair_halves(r[:128], r[128:])
    scatter(a_out, a_in, ass, asr)
    quarter = lane_iota((128, 128)) // 32
    names = 0.0
    for r in range(4):
        picked = bdot(hot_ref[128 * r : 128 * r + 128], wcol[...].astype(BF16))
        names = names + jnp.where(quarter == r, picked, 0.0)
    l_out[...] = names.reshape(128, 1, 128)
    scatter(l_out, l_in, qss, qsr)
    settle(a_out, a_in, asr)

    for i in range(8):
        for h in range(2):
            vals = swap_groups([a_in[i * 16 + h * 8 + k] for k in range(8)], 16)
            for k in range(8):
                row = (k // 4) * 256 + i * 32 + (k % 4) * 8
                m_ref[row : row + 8, 128 * h : 128 * h + 128] = vals[k]
    tzs, lxs = (tz[0], tz[1]), (lx[0], lx[1])
    b = dot3(split2(m_ref[...]), tzs)
    scale = SECOND_ORDER / (N * N * N)
    halves = []
    for q in range(2):
        c = dot3(lxs, split2(b[256 * q : 256 * q + 256]))
        eigen = tab[2] + lap_ref[me + 128 * q]
        anchor = eigen == 0.0
        c = c * jnp.where(anchor, 0.0, scale / jnp.where(anchor, -1.0, eigen))
        halves.append(hdot(tab[1], c))
    m_ref[...] = hdot(jnp.concatenate(halves, axis=0), tab[0])
    for i in range(8):
        for h in range(2):
            vals = []
            for k in range(8):
                row = (k // 4) * 256 + i * 32 + (k % 4) * 8
                vals.append(m_ref[row : row + 8, 128 * h : 128 * h + 128])
            vals = swap_groups(vals, 16)
            for k in range(8):
                b_out[i * 16 + h * 8 + k] = vals[k]
    scatter(b_out, b_in, bss, bsr)
    settle(b_out, b_in, bsr)
    for h in range(4):
        a = jnp.concatenate(pair_halves(b_in[:, 2 * h, :], b_in[:, 2 * h + 1, :]), axis=0)
        phi[8 * h + 1 : 8 * h + 9] = pp[8 * h + 1 : 8 * h + 9] + hdot(a.T, tab[0]).reshape(8, 16, N)
    fys[0] = phi[1:33, 15, :]
    fys[1] = phi[1:33, 0, :]
    copies = [
        near(0, phi.at[32], phi.at[0], fss, fsr),
        near(1, phi.at[1], phi.at[33], fss, fsr),
        near(2, fys.at[0], fyr.at[0], fss, fsr),
        near(3, fys.at[1], fyr.at[1], fss, fsr),
    ]
    loads[2].wait()
    loads[3].wait()

    def chosen(ft, sel):
        out = 0.0
        for part in split3(jnp.concatenate([ft[pl.ds(e, 32, stride=8), :] for e in range(8)], axis=0)):
            out = out + bdot(part, sel)
        return out

    for m in range(4):
        ft_all[m] = phi[8 * m + 1 : 8 * m + 9].reshape(128, N).T
        w_ref[:, 256 * m : 256 * m + 256] = chosen(ft_all.at[m], sel_ref[0:128])
    for copy in copies:
        copy.wait()
    w = []
    for m in range(4):
        faces = jnp.concatenate(
            [phi[8 * m], phi[8 * m + 9], fyr[0, 8 * m : 8 * m + 8], fyr[1, 8 * m : 8 * m + 8], jnp.zeros((80, N), F32)],
            axis=0,
        )
        ft_all[m] = faces.T
        w.append(w_ref[:, 256 * m : 256 * m + 256] + chosen(ft_all.at[m], sel_ref[128:256]))
    w = jnp.concatenate(w, axis=1)

    def slab(e, turn):
        rows = w[32 * e : 32 * e + 32]
        if turn:
            rows = pltpu.roll(rows, turn, 0)
        return jnp.concatenate([rows[:, 128 * g : 128 * g + 128] for g in range(8)], axis=0)

    zfaces = (slab(7, 1), slab(0, 31))
    lanes = lane_iota((256, 128))
    hot = hot_ref[...]

    def full(k):
        face = pltpu.roll(zfaces[k // 4], 96 - 16 * (k % 4), 1)
        return jnp.where(lanes >= 96, face, slab(k, 0))

    last = full(7)
    parts = []
    for e in range(0, 7, 2):
        pair = []
        for k in range(e, min(e + 2, 7)):
            tail = pltpu.roll(last, 112 - 16 * k, 1)
            pair.append(jnp.where(lanes >= 112, tail, full(k)))
        parts.append(split3(jnp.concatenate(pair, axis=1)))

    def place(first, count):
        rows = hot[128 * first : 128 * (first + count)]
        for k, (a, b, c) in enumerate(parts):
            o = bdot(rows, a) + bdot(rows, b) + bdot(rows, c)
            for r in range(count):
                c_out[first + r, :, 2 * k, :] = o[128 * r : 128 * r + 128, :128]
                if k < 3:
                    c_out[first + r, :, 2 * k + 1, :] = o[128 * r : 128 * r + 128, 128:]

    place(0, 1)
    scatter(c_out.at[0], c_in.at[0], css.at[0], csr.at[0])
    place(1, 3)
    scatter(c_out.at[1], c_in.at[1], css.at[1], csr.at[1])
    settle(l_out, l_in, qsr)
    ids = lane_iota((128, 256)).astype(F32) + 1.0
    for r in range(4):
        label = l_in[...].reshape(128, 128)[:, 32 * r : 32 * r + 1]
        named_ref[r] = (jnp.broadcast_to(label, (128, 256)) == ids).astype(F32).astype(BF16)
    g_ref[...] = jnp.zeros_like(g_ref)
    sub = lax.broadcasted_iota(jnp.int32, (8, 8, 128), 1)
    sub5 = lax.broadcasted_iota(jnp.int32, (8, 128), 0)

    def chunk(r, carry):
        settle(c_out.at[r], c_in.at[r], csr.at[r])

        @pl.when(r < 2)
        def _():
            scatter(c_out.at[r + 2], c_in.at[r + 2], css.at[r + 2], csr.at[r + 2])

        for e in range(7):
            ct_ref[e] = c_in[r, :, e, :].T
            ct_ref[7, 16 * e : 16 * e + 16] = ct_ref[e, 112:128]
        for e in range(8):
            cp[e + 1, 1:9] = ct_ref[e, 0:64].reshape(8, 8, 128)
            cp[e + 1, 0] = ct_ref[e, 64:72]
            cp[e + 1, 9] = ct_ref[e, 72:80]
            k = 1 + 2 * (e % 4)
            cp[9 * (e // 4), k : k + 2] = ct_ref[e, 96:112].reshape(2, 8, 128)

        def taps(e, carry):
            f = cp[e + 1, 1:9]
            ym = jnp.stack([jnp.broadcast_to(ct_ref[e, 80 + k : 81 + k], (8, 128)) for k in range(8)])
            yp = jnp.stack([jnp.broadcast_to(ct_ref[e, 88 + k : 89 + k], (8, 128)) for k in range(8)])
            ym = jnp.where(sub == 0, ym, pltpu.roll(f, 1, 1))
            yp = jnp.where(sub == 7, yp, pltpu.roll(f, 7, 1))
            triples = (
                (wx_ref, cp[e + 1, 0:8], cp[e + 1, 2:10]),
                (wy_ref, ym, yp),
                (wz_ref, cp[e, 1:9], cp[e + 2, 1:9]),
            )
            for ref, lo, hi in triples:
                for d, tap in enumerate(spline_taps((lo - hi) * 0.5)):
                    ref[d, e] = tap
            return carry

        lax.fori_loop(0, 8, taps, 0)
        for u in range(12):
            acc = [None] * 12
            for e in range(8):
                for a in range(max(0, u - 4), min(8, u + 1)):
                    q = wx_ref[u - a, e, a][None] * wy_ref[:, e, a]
                    for dz in range(5):
                        v = q * wz_ref[dz, e, a][None]
                        k = e + dz
                        acc[k] = v if acc[k] is None else acc[k] + v
                for k in [e] if e < 7 else range(7, 12):
                    turned = [pltpu.roll(acc[k][dy], dy, 0) for dy in range(1, 5)]
                    over = [jnp.where(sub5 < dy, t, 0.0) for dy, t in enumerate(turned, 1)]
                    hi = (over[0] + over[1]) + (over[2] + over[3])
                    d_ref[k, u, 0:8, :] = acc[k][0] + (turned[0] + turned[1]) + (turned[2] + turned[3]) - hi
                    d_ref[k, u, 8:16, :] = hi

        named = named_ref[r]
        for k in range(12):
            a, b = split2(d_ref[k].reshape(192, 128))
            o = bdot(a, named) + bdot(b, named)
            g_ref[k] = g_ref[k] + o
        return carry

    lax.fori_loop(0, 4, chunk, 0)
    for half in range(2):
        for k in range(3):
            vals = [g_ref[4 * k + m][:, 128 * half : 128 * half + 128] for m in range(4)]
            vals = swap_groups(vals, 32)
            for gl in range(4):
                h_ref[half * 4 + gl, :, 128 * k : 128 * k + 128] = vals[gl]
    tile[...] = jnp.zeros_like(tile)
    sp = sp_ref[...]
    for g in range(8):
        a, b = split2(h_ref[g])
        o = (bdot(a, sp) + bdot(b, sp)).reshape(12, 16, N)
        bx, by = g // 2, g % 2
        tile[8 * bx : 8 * bx + 12, 8 * by : 8 * by + 16, :] += o
    for k in range(2):
        rys[0, k] = tile[2:34, 18 + k, :]
        rys[1, k] = tile[2:34, k, :]
    copies = [
        near(0, tile.at[pl.ds(34, 2)], rxr.at[0], rss, rsr),
        near(1, tile.at[pl.ds(0, 2)], rxr.at[1], rss, rsr),
        near(2, rys.at[0], ryr.at[0], rss, rsr),
        near(3, rys.at[1], ryr.at[1], rss, rsr),
        near(4, tile.at[pl.ds(34, 2), pl.ds(16, 8)], rcr.at[0], rss, rsr),
        near(5, tile.at[pl.ds(34, 2), pl.ds(0, 8)], rcr.at[1], rss, rsr),
        near(6, tile.at[pl.ds(0, 2), pl.ds(16, 8)], rcr.at[2], rss, rsr),
        near(7, tile.at[pl.ds(0, 2), pl.ds(0, 8)], rcr.at[3], rss, rsr),
    ]
    dens_ref[...] = tile[2:34, 2:18, :]
    for copy in copies:
        copy.wait()
    dens_ref[0:2] += rxr[0, :, 2:18, :]
    dens_ref[30:32] += rxr[1, :, 2:18, :]
    for k in range(2):
        dens_ref[:, k, :] += ryr[0, k]
        dens_ref[:, 14 + k, :] += ryr[1, k]
    dens_ref[0:2, 0:2] += rcr[0, :, 2:4]
    dens_ref[0:2, 14:16] += rcr[1, :, 0:2]
    dens_ref[30:32, 0:2] += rcr[2, :, 2:4]
    dens_ref[30:32, 14:16] += rcr[3, :, 0:2]
    settle(a_out, a_in, ass)
    settle(l_out, l_in, qss)
    settle(b_out, b_in, bss)
    for r in range(4):
        settle(c_out.at[r], c_in.at[r], css.at[r])


def finish_kernel(phi, fyr, dens, disp_ref, out_ref, buf, sem):
    copies = [pltpu.make_async_copy(dens, out_ref, sem.at[4])]
    copies[0].start()
    for g in range(4):
        for x in range(8 * g, 8 * g + 8):
            f = phi[x + 1]
            up, down = shift_rows(f, fyr[0, x : x + 1], fyr[1, x : x + 1])
            buf[0, x] = (phi[x] - phi[x + 2]) * 0.5
            buf[1, x] = (down - up) * 0.5
            buf[2, x] = (pltpu.roll(f, 1, 1) - pltpu.roll(f, N - 1, 1)) * 0.5
        part = pl.ds(8 * g, 8)
        copies.append(pltpu.make_async_copy(buf.at[:, part], disp_ref.at[:, part], sem.at[g]))
        copies[-1].start()
    for copy in copies:
        copy.wait()


def vm(*shape):
    return pltpu.VMEM(shape, F32)


def sds(*shape):
    return jax.ShapeDtypeStruct(shape, F32)


def per_device(potential, owner, window):
    dma = pltpu.SemaphoreType.DMA
    scratch = [
        vm(34, 16, N), vm(3, N, N), pltpu.VMEM((N, N), BF16), pltpu.VMEM((384, N), BF16),
        pltpu.VMEM((2, N, N), BF16), pltpu.VMEM((2, N, N), BF16), pltpu.VMEM((512, N), BF16), vm(N, 128),
        vm(4, N, 128), vm(N, 1024), vm(2, 32, N), vm(2, 32, N), vm(4, 8, N), vm(2, 40, N), vm(32, 16, N),
        vm(128, 8, 128), vm(128, 8, 128), vm(512, N), vm(128, 8, 128), vm(128, 8, 128), vm(2, 32, N),
        vm(4, 128, 7, 128), vm(4, 128, 7, 128), vm(128, 1, 128), vm(128, 1, 128), pltpu.VMEM((4, 128, N), BF16),
        vm(8, 128, 128), vm(10, 10, 8, 128),
        vm(5, 8, 8, 8, 128), vm(5, 8, 8, 8, 128), vm(5, 8, 8, 8, 128),
        vm(12, 12, 16, 128), vm(12, 192, N), vm(8, 192, 384), vm(36, 24, N),
        vm(2, 2, 24, N), vm(2, 2, 32, N), vm(2, 2, 32, N), vm(4, 2, 8, N),
        dma((4,)), dma((8,)), dma((8,)), dma((4,)), dma((4,)), dma((8,)), dma((8,)),
        dma, dma, dma, dma, dma((4,)), dma((4,)), dma, dma,
    ]
    vmem = pl.BlockSpec(memory_space=pltpu.VMEM)
    hbm = pl.BlockSpec(memory_space=pl.ANY)
    phi, sides, dens = pl.pallas_call(
        whole_kernel,
        out_shape=[sds(34, 16, N), sds(2, 32, N), sds(32, 16, N)],
        in_specs=[pl.BlockSpec(memory_space=pltpu.SMEM), vmem, vmem, hbm, hbm, hbm, hbm],
        out_specs=[vmem, vmem, vmem],
        scratch_shapes=scratch,
        compiler_params=pltpu.CompilerParams(vmem_limit_bytes=VLIM, collective_id=0, has_side_effects=True),
    )(
        jnp.asarray(LAP), owner.reshape(1, 256), window.reshape(1, 256), potential, jnp.asarray(TABLES),
        jnp.asarray(SELECT, BF16), jnp.asarray(SPREAD, BF16),
    )
    return pl.pallas_call(
        finish_kernel,
        out_shape=[sds(3, 32, 16, N), sds(32, 16, N)],
        in_specs=[vmem, vmem, vmem],
        out_specs=[hbm, hbm],
        scratch_shapes=[vm(3, 32, 16, N), dma((5,))],
        compiler_params=pltpu.CompilerParams(vmem_limit_bytes=VLIM),
    )(phi, sides, dens)


def solution(mesh):
    return jax.shard_map(
        per_device,
        mesh=mesh,
        in_specs=(P("px", "py", None), P("px", "py", None, None), P("px", "py", None)),
        out_specs=(P(None, "px", "py", None), P("px", "py", None)),
        check_vma=False,
    )
```

```python
import functools
import math

import jax
import jax.numpy as jnp
import numpy as np
from jax import lax
from jax.experimental import pallas as pl
from jax.experimental.pallas import tpu as pltpu
from jax.sharding import PartitionSpec as P

SECOND_ORDER = 3.0 / 7.0
HIGHEST = lax.Precision.HIGHEST
F32 = jnp.float32
BF16 = jnp.bfloat16
N = 256
VLIM = 60 * 1024 * 1024


def cas_table(a, b):
    angle = (np.multiply.outer(a, b) % N) * (2.0 * math.pi / N)
    return np.cos(angle) + np.sin(angle)


def constants():
    n = np.arange(N)
    r = np.arange(N)
    x = 32 * (r // 32) + 4 * (r % 8) + r // 8 % 4
    lap = -4.0 * np.sin(math.pi * n / N) ** 2
    tables = np.stack([cas_table(n, n), cas_table(x, x), lap[x][:, None] + lap[None, :]])
    return tables.astype(np.float32), lap.astype(np.float32)


def block_select():
    sel = np.zeros((256, 2, 128), np.float32)
    for by in range(2):
        for a in range(8):
            for c in range(8):
                sel[a * 16 + 8 * by + c, by, a * 8 + c] = 1.0
            sel[160 + a if by == 0 else a * 16 + 7, by, 80 + a] = 1.0
            sel[a * 16 + 8 if by == 0 else 168 + a, by, 88 + a] = 1.0
        for c in range(8):
            sel[128 + 8 * by + c, by, 64 + c] = 1.0
            sel[144 + 8 * by + c, by, 72 + c] = 1.0
    return sel.reshape(256, 256)


def spread_z():
    sel = np.zeros((12, 32, N), np.float32)
    for s in range(12):
        for b in range(32):
            sel[s, b, (8 * b + s - 2) % N] = 1.0
    return sel.reshape(384, N)


TABLES, LAP = constants()
SELECT = block_select()
SPREAD = spread_z()


def lane_iota(shape):
    return lax.broadcasted_iota(jnp.int32, shape, len(shape) - 1)


def swap_groups(vals, width):
    count = len(vals)
    group = lane_iota(vals[0].shape) // width
    turned = [pltpu.roll(v, k * width, 1) if k else v for k, v in enumerate(vals)]
    step = 1
    while step < count:
        high = (group & step) != 0
        turned = [jnp.where(high, turned[(k + step) % count], turned[k]) for k in range(count)]
        step *= 2
    return [pltpu.roll(turned[-k % count], 128 - k * width, 1) if k else turned[0] for k in range(count)]


def split3(x):
    a = x.astype(BF16)
    r = x - a.astype(F32)
    b = r.astype(BF16)
    c = (r - b.astype(F32)).astype(BF16)
    return a, b, c


def split2(x):
    a = x.astype(BF16)
    return a, (x - a.astype(F32)).astype(BF16)


def bdot(a, b):
    return jnp.dot(a, b, preferred_element_type=F32)


MESH = pl.DeviceIdType.MESH


def torus_rings():
    rings = [[] for _ in range(7)]
    for a in range(4):
        for b in range(4):
            for d in range(4):
                rings[sum(min(o, 4 - o) for o in (a, b, d))].append((a, b, d))
    return rings[::-1]


RINGS = torus_rings()
STEPS = ((1, 0), (-1, 0), (0, 1), (0, -1), (1, 1), (1, -1), (-1, 1), (-1, -1))
hdot = functools.partial(jnp.dot, precision=HIGHEST, preferred_element_type=F32)


def dot3(a, b):
    return bdot(a[0], b[0]) + (bdot(a[0], b[1]) + bdot(a[1], b[0]))


def rows_dot3(a, b):
    def one(x, y):
        return lax.dot_general(x, y, (((1,), (1,)), ((), ())), preferred_element_type=F32)

    return one(a[0], b[0]) + (one(a[0], b[1]) + one(a[1], b[0]))


def pair_halves(a, b):
    low = lane_iota(a.shape) < 64
    return jnp.where(low, a, pltpu.roll(b, 64, 1)), jnp.where(low, pltpu.roll(a, 64, 1), b)


def shift_rows(p, before, after):
    up = jnp.concatenate([p[1:], after], axis=0)
    down = jnp.concatenate([before, p[:-1]], axis=0)
    return up, down


def spline_taps(t):
    t = jnp.clip(t, -1.0, 1.0)
    up = jnp.maximum(t, 0.0)
    dn = up - t
    p3 = up * up * up * (1.0 / 6.0)
    n3 = dn * dn * dn * (1.0 / 6.0)
    sq = t * t
    both = p3 + n3
    base = sq * 0.5 + (1.0 / 6.0) - both
    half = t * 0.5
    return n3, base - half - 2.0 * n3, (2.0 / 3.0) - sq + 3.0 * both, base + half - 2.0 * p3, p3


def whole_kernel(
    lap_hbm, own_hbm, win_hbm, p_hbm, tab_hbm, sel_hbm, sp_hbm,
    disp_hbm, dens_ref,
    lap_ref, orow_ref, wrow_ref, inv_ref, phi, fyr, buf, pp, tab, sel_ref, sp_ref, tz, lx, hot_ref, wcol,
    ft_all, w_ref, pys, pyr, pcr, yl, src, a_out, a_in, m_ref, b_out, b_in, fys,
    c_out, c_in, l_out, l_in, named_ref, ct_ref, cp, wx_ref, wy_ref, wz_ref, d_ref, g_ref, h_ref, tile, rxr, rys, ryr, rcr,
    lsem, hss, hsr, fss, fsr, rss, rsr, ass, asr, bss, bsr, css, csr, qss, qsr,
):
    ix, iy = lax.axis_index("px"), lax.axis_index("py")
    me = ix * 16 + iy
    barrier = pltpu.get_barrier_semaphore()

    cx, core, cy, cz = ix // 2, lax.rem(ix, 2), iy // 4, lax.rem(iy, 4)

    def each_peer(act):
        for offsets in RINGS:

            def ring(n, carry, offsets=offsets):
                side = lax.rem(core + n + 1, 2)
                for a, b, d in offsets:
                    act(lax.rem(cx + a, 4) * 2 + side, lax.rem(cy + b, 4) * 4 + lax.rem(cz + d, 4))
                return carry

            lax.fori_loop(0, 2 if offsets[0] != (0, 0, 0) else 1, ring, 0)

    def greet(px, py):
        pl.semaphore_signal(barrier, 1, device_id=(px, py), device_id_type=MESH)

    each_peer(greet)

    def near(k, source, dest, ssem, rsem):
        dx, dy = STEPS[k]
        where = (lax.rem(ix + dx + 8, 8), lax.rem(iy + dy + 16, 16))
        copy = pltpu.make_async_remote_copy(
            source, dest, ssem.at[k], rsem.at[k], device_id=where, device_id_type=MESH
        )
        copy.start()
        return copy

    def scatter(out, into, ssem, rsem):
        def send(px, py):
            pltpu.make_async_remote_copy(
                out.at[px * 16 + py], into.at[me], ssem, rsem, device_id=(px, py), device_id_type=MESH
            ).start()

        each_peer(send)
        into[me] = out[me]

    def settle(out, into, sem):
        pltpu.make_async_copy(out.at[pl.ds(0, 127)], into.at[pl.ds(0, 127)], sem).wait()

    loads = [
        pltpu.make_async_copy(p_hbm, pp.at[pl.ds(1, 32)], lsem.at[0]),
        pltpu.make_async_copy(tab_hbm, tab, lsem.at[1]),
        pltpu.make_async_copy(sel_hbm, sel_ref, lsem.at[2]),
        pltpu.make_async_copy(sp_hbm, sp_ref, lsem.at[3]),
        pltpu.make_async_copy(lap_hbm, lap_ref, lsem.at[5]),
        pltpu.make_async_copy(own_hbm, orow_ref, lsem.at[6]),
        pltpu.make_async_copy(win_hbm, wrow_ref, lsem.at[7]),
    ]
    for load in loads:
        load.start()
    loads[0].wait()
    pys[0] = pp[1:33, 15, :]
    pys[1] = pp[1:33, 0, :]
    pl.semaphore_wait(barrier, 127)
    copies = [
        near(0, pp.at[32], pp.at[0], hss, hsr),
        near(1, pp.at[1], pp.at[33], hss, hsr),
        near(2, pys.at[0], pyr.at[0], hss, hsr),
        near(3, pys.at[1], pyr.at[1], hss, hsr),
        near(4, pp.at[32, pl.ds(8, 8)], pcr.at[0], hss, hsr),
        near(5, pp.at[32, pl.ds(0, 8)], pcr.at[1], hss, hsr),
        near(6, pp.at[1, pl.ds(8, 8)], pcr.at[2], hss, hsr),
        near(7, pp.at[1, pl.ds(0, 8)], pcr.at[3], hss, hsr),
    ]
    loads[1].wait()
    tz[0], tz[1] = split2(tab[0])
    lx[0], lx[1] = split2(tab[1])
    for copy in copies:
        copy.wait()
    yl[0, 0:1] = pcr[0, 7:8]
    yl[0, 1:33] = pyr[0]
    yl[0, 33:34] = pcr[2, 7:8]
    yl[1, 0:1] = pcr[1, 0:1]
    yl[1, 1:33] = pyr[1]
    yl[1, 33:34] = pcr[3, 0:1]

    planes = []
    for x in range(34):
        p = pp[x]
        up, down = shift_rows(p, yl[0, x : x + 1], yl[1, x : x + 1])
        ahead, behind = pltpu.roll(p, N - 1, 1), pltpu.roll(p, 1, 1)
        planes.append((p, up - down, ahead - behind, up + down - 2.0 * p, ahead + behind - 2.0 * p))
        if x < 2:
            continue
        (p0, dy0, dz0, _, _), (p1, dy1, _, yy, zz), (p2, dy2, dz2, _, _) = planes[-3:]
        xx = p2 - 2.0 * p1 + p0
        xy, xz = dy2 - dy0, dz2 - dz0
        yz = pltpu.roll(dy1, N - 1, 1) - pltpu.roll(dy1, 1, 1)
        src[x - 2] = xx * (yy + zz) + yy * zz - (xy * xy + xz * xz + yz * yz) * 0.0625
        if x % 8 == 1:
            h = x // 8 - 1
            part = split2(src[8 * h : 8 * h + 8].reshape(128, N))
            r = rows_dot3((tz[0], tz[1]), part)
            a_out[:, 2 * h, :], a_out[:, 2 * h + 1, :] = pair_halves(r[:128], r[128:])
    scatter(a_out, a_in, ass, asr)
    for load in loads[4:]:
        load.wait()
    wide = jnp.broadcast_to(orow_ref[...].astype(F32), (256, 256))
    r_i = lax.broadcasted_iota(jnp.int32, (256, 256), 0)
    c_i = lax.broadcasted_iota(jnp.int32, (256, 256), 1)
    same = jnp.where((wide.T == wide) & (r_i < c_i), 1, 0)
    slot = jnp.sum(same, axis=0, keepdims=True) * 128 + orow_ref[...]
    hot_ref[...] = (lax.broadcasted_iota(jnp.int32, (512, 256), 0) == slot).astype(F32).astype(BF16)
    wcol[...] = jnp.broadcast_to(wrow_ref[...].astype(F32) + 1.0, (128, 256)).T
    quarter = lane_iota((128, 128)) // 32
    names = 0.0
    for r in range(4):
        picked = bdot(hot_ref[128 * r : 128 * r + 128], wcol[...].astype(BF16))
        names = names + jnp.where(quarter == r, picked, 0.0)
    l_out[...] = names.reshape(128, 1, 128)
    scatter(l_out, l_in, qss, qsr)
    scale = SECOND_ORDER / (N * N * N)
    for q in range(2):
        eigen = tab[2] + lap_ref[me + 128 * q]
        anchor = eigen == 0.0
        inv_ref[q] = jnp.where(anchor, 0.0, scale / jnp.where(anchor, -1.0, eigen))
    settle(a_out, a_in, asr)

    for i in range(8):
        for h in range(2):
            vals = swap_groups([a_in[i * 16 + h * 8 + k] for k in range(8)], 16)
            for k in range(8):
                row = (k // 4) * 256 + i * 32 + (k % 4) * 8
                m_ref[row : row + 8, 128 * h : 128 * h + 128] = vals[k]
    tzs, lxs = (tz[0], tz[1]), (lx[0], lx[1])
    b = dot3(split2(m_ref[...]), tzs)
    halves = []
    for q in range(2):
        c = dot3(lxs, split2(b[256 * q : 256 * q + 256]))
        c = c * inv_ref[q]
        halves.append(hdot(tab[1], c))
    m_ref[...] = hdot(jnp.concatenate(halves, axis=0), tab[0])
    for i in range(8):
        for h in range(2):
            vals = []
            for k in range(8):
                row = (k // 4) * 256 + i * 32 + (k % 4) * 8
                vals.append(m_ref[row : row + 8, 128 * h : 128 * h + 128])
            vals = swap_groups(vals, 16)
            for k in range(8):
                b_out[i * 16 + h * 8 + k] = vals[k]
    scatter(b_out, b_in, bss, bsr)
    settle(b_out, b_in, bsr)
    for h in range(4):
        a = jnp.concatenate(pair_halves(b_in[:, 2 * h, :], b_in[:, 2 * h + 1, :]), axis=0)
        phi[8 * h + 1 : 8 * h + 9] = pp[8 * h + 1 : 8 * h + 9] + hdot(a.T, tab[0]).reshape(8, 16, N)
    fys[0] = phi[1:33, 15, :]
    fys[1] = phi[1:33, 0, :]
    copies = [
        near(0, phi.at[32], phi.at[0], fss, fsr),
        near(1, phi.at[1], phi.at[33], fss, fsr),
        near(2, fys.at[0], fyr.at[0], fss, fsr),
        near(3, fys.at[1], fyr.at[1], fss, fsr),
    ]
    loads[2].wait()
    loads[3].wait()

    def chosen(ft, sel):
        out = 0.0
        for part in split3(jnp.concatenate([ft[pl.ds(e, 32, stride=8), :] for e in range(8)], axis=0)):
            out = out + bdot(part, sel)
        return out

    for m in range(4):
        ft_all[m] = phi[8 * m + 1 : 8 * m + 9].reshape(128, N).T
        w_ref[:, 256 * m : 256 * m + 256] = chosen(ft_all.at[m], sel_ref[0:128])
    for copy in copies:
        copy.wait()
    w = []
    for m in range(4):
        faces = jnp.concatenate(
            [phi[8 * m], phi[8 * m + 9], fyr[0, 8 * m : 8 * m + 8], fyr[1, 8 * m : 8 * m + 8], jnp.zeros((80, N), F32)],
            axis=0,
        )
        ft_all[m] = faces.T
        w.append(w_ref[:, 256 * m : 256 * m + 256] + chosen(ft_all.at[m], sel_ref[128:256]))
    w = jnp.concatenate(w, axis=1)

    def slab(e, turn):
        rows = w[32 * e : 32 * e + 32]
        if turn:
            rows = pltpu.roll(rows, turn, 0)
        return jnp.concatenate([rows[:, 128 * g : 128 * g + 128] for g in range(8)], axis=0)

    zfaces = (slab(7, 1), slab(0, 31))
    lanes = lane_iota((256, 128))
    hot = hot_ref[...]

    def full(k):
        face = pltpu.roll(zfaces[k // 4], 96 - 16 * (k % 4), 1)
        return jnp.where(lanes >= 96, face, slab(k, 0))

    last = full(7)
    parts = []
    for e in range(0, 7, 2):
        pair = []
        for k in range(e, min(e + 2, 7)):
            tail = pltpu.roll(last, 112 - 16 * k, 1)
            pair.append(jnp.where(lanes >= 112, tail, full(k)))
        parts.append(split3(jnp.concatenate(pair, axis=1)))

    def place(first, count):
        rows = hot[128 * first : 128 * (first + count)]
        for k, (a, b, c) in enumerate(parts):
            o = bdot(rows, a) + bdot(rows, b) + bdot(rows, c)
            for r in range(count):
                c_out[first + r, :, 2 * k, :] = o[128 * r : 128 * r + 128, :128]
                if k < 3:
                    c_out[first + r, :, 2 * k + 1, :] = o[128 * r : 128 * r + 128, 128:]

    place(0, 1)
    scatter(c_out.at[0], c_in.at[0], css.at[0], csr.at[0])
    place(1, 3)
    scatter(c_out.at[1], c_in.at[1], css.at[1], csr.at[1])
    settle(l_out, l_in, qsr)
    ids = lane_iota((128, 256)).astype(F32) + 1.0
    for r in range(4):
        label = l_in[...].reshape(128, 128)[:, 32 * r : 32 * r + 1]
        named_ref[r] = (jnp.broadcast_to(label, (128, 256)) == ids).astype(F32).astype(BF16)
    scatter(c_out.at[2], c_in.at[2], css.at[2], csr.at[2])
    for x in range(32):
        f = phi[x + 1]
        up, down = shift_rows(f, fyr[0, x : x + 1], fyr[1, x : x + 1])
        buf[0, x] = (phi[x] - phi[x + 2]) * 0.5
        buf[1, x] = (down - up) * 0.5
        buf[2, x] = (pltpu.roll(f, 1, 1) - pltpu.roll(f, N - 1, 1)) * 0.5
    stored = pltpu.make_async_copy(buf, disp_hbm, lsem.at[4])
    stored.start()
    scatter(c_out.at[3], c_in.at[3], css.at[3], csr.at[3])
    sub = lax.broadcasted_iota(jnp.int32, (8, 8, 128), 1)
    sub5 = lax.broadcasted_iota(jnp.int32, (8, 128), 0)

    def chunk(r, slot):
        settle(c_out.at[r], c_in.at[r], csr.at[r])

        for e in range(7):
            ct_ref[e] = c_in[r, :, e, :].T
            ct_ref[7, 16 * e : 16 * e + 16] = ct_ref[e, 112:128]
        for e in range(8):
            cp[e + 1, 1:9] = ct_ref[e, 0:64].reshape(8, 8, 128)
            cp[e + 1, 0] = ct_ref[e, 64:72]
            cp[e + 1, 9] = ct_ref[e, 72:80]
            k = 1 + 2 * (e % 4)
            cp[9 * (e // 4), k : k + 2] = ct_ref[e, 96:112].reshape(2, 8, 128)

        def taps(e, carry):
            f = cp[e + 1, 1:9]
            ym = jnp.stack([jnp.broadcast_to(ct_ref[e, 80 + k : 81 + k], (8, 128)) for k in range(8)])
            yp = jnp.stack([jnp.broadcast_to(ct_ref[e, 88 + k : 89 + k], (8, 128)) for k in range(8)])
            ym = jnp.where(sub == 0, ym, pltpu.roll(f, 1, 1))
            yp = jnp.where(sub == 7, yp, pltpu.roll(f, 7, 1))
            triples = (
                (wx_ref, cp[e + 1, 0:8], cp[e + 1, 2:10]),
                (wy_ref, ym, yp),
                (wz_ref, cp[e, 1:9], cp[e + 2, 1:9]),
            )
            for ref, lo, hi in triples:
                for d, tap in enumerate(spline_taps((lo - hi) * 0.5)):
                    ref[d, e] = tap
            return carry

        lax.fori_loop(0, 8, taps, 0)
        for u in range(12):
            acc = [None] * 12
            for e in range(8):
                for a in range(max(0, u - 4), min(8, u + 1)):
                    q = wx_ref[u - a, e, a][None] * wy_ref[:, e, a]
                    for dz in range(5):
                        v = q * wz_ref[dz, e, a][None]
                        k = e + dz
                        acc[k] = v if acc[k] is None else acc[k] + v
                for k in [e] if e < 7 else range(7, 12):
                    turned = [pltpu.roll(acc[k][dy], dy, 0) for dy in range(1, 5)]
                    over = [jnp.where(sub5 < dy, t, 0.0) for dy, t in enumerate(turned, 1)]
                    hi = (over[0] + over[1]) + (over[2] + over[3])
                    d_ref[k, slot, u, 0:8, :] = acc[k][0] + (turned[0] + turned[1]) + (turned[2] + turned[3]) - hi
                    d_ref[k, slot, u, 8:16, :] = hi

    def pair(n, carry):
        for r in range(2):
            chunk(2 * n + r, r)
        named = jnp.concatenate([named_ref[2 * n], named_ref[2 * n + 1]], axis=0)
        for k in range(12):
            a, b = split2(jnp.concatenate([d_ref[k, r].reshape(192, 128) for r in range(2)], axis=1))
            g_ref[k] = g_ref[k] + (bdot(a, named) + bdot(b, named))
        return carry

    g_ref[...] = jnp.zeros_like(g_ref)
    lax.fori_loop(0, 2, pair, 0)
    for half in range(2):
        for k in range(3):
            vals = [g_ref[4 * k + m][:, 128 * half : 128 * half + 128] for m in range(4)]
            vals = swap_groups(vals, 32)
            for gl in range(4):
                h_ref[half * 4 + gl, :, 128 * k : 128 * k + 128] = vals[gl]
    tile[...] = jnp.zeros_like(tile)
    sp = sp_ref[...]
    for g in range(8):
        a, b = split2(h_ref[g])
        o = (bdot(a, sp) + bdot(b, sp)).reshape(12, 16, N)
        bx, by = g // 2, g % 2
        tile[8 * bx : 8 * bx + 12, 8 * by : 8 * by + 16, :] += o
    for k in range(2):
        rys[0, k] = tile[2:34, 18 + k, :]
        rys[1, k] = tile[2:34, k, :]
    copies = [
        near(0, tile.at[pl.ds(34, 2)], rxr.at[0], rss, rsr),
        near(1, tile.at[pl.ds(0, 2)], rxr.at[1], rss, rsr),
        near(2, rys.at[0], ryr.at[0], rss, rsr),
        near(3, rys.at[1], ryr.at[1], rss, rsr),
        near(4, tile.at[pl.ds(34, 2), pl.ds(16, 8)], rcr.at[0], rss, rsr),
        near(5, tile.at[pl.ds(34, 2), pl.ds(0, 8)], rcr.at[1], rss, rsr),
        near(6, tile.at[pl.ds(0, 2), pl.ds(16, 8)], rcr.at[2], rss, rsr),
        near(7, tile.at[pl.ds(0, 2), pl.ds(0, 8)], rcr.at[3], rss, rsr),
    ]
    dens_ref[...] = tile[2:34, 2:18, :]
    for copy in copies:
        copy.wait()
    dens_ref[0:2] += rxr[0, :, 2:18, :]
    dens_ref[30:32] += rxr[1, :, 2:18, :]
    for k in range(2):
        dens_ref[:, k, :] += ryr[0, k]
        dens_ref[:, 14 + k, :] += ryr[1, k]
    dens_ref[0:2, 0:2] += rcr[0, :, 2:4]
    dens_ref[0:2, 14:16] += rcr[1, :, 0:2]
    dens_ref[30:32, 0:2] += rcr[2, :, 2:4]
    dens_ref[30:32, 14:16] += rcr[3, :, 0:2]
    stored.wait()
    settle(a_out, a_in, ass)
    settle(l_out, l_in, qss)
    settle(b_out, b_in, bss)
    for r in range(4):
        settle(c_out.at[r], c_in.at[r], css.at[r])


def finish_kernel(disp, dens, disp_out, dens_out, buf, isem, osem):
    into, out = [], []
    for g in range(4):
        part = pl.ds(8 * g, 8)
        slots = buf.at[:, part]
        into.append(pltpu.make_async_copy(disp.at[:, part], slots.at[0:3], isem.at[g, 0]))
        into.append(pltpu.make_async_copy(dens.at[part], slots.at[3], isem.at[g, 1]))
        out.append(pltpu.make_async_copy(slots.at[0:3], disp_out.at[:, part], osem.at[g, 0]))
        out.append(pltpu.make_async_copy(slots.at[3], dens_out.at[part], osem.at[g, 1]))
    for copy in into:
        copy.start()
    for a, b in zip(into, out):
        a.wait()
        b.start()
    for copy in out:
        copy.wait()


def vm(*shape):
    return pltpu.VMEM(shape, F32)


def sds(*shape):
    return jax.ShapeDtypeStruct(shape, F32)


def per_device(potential, owner, window):
    dma = pltpu.SemaphoreType.DMA
    scratch = [
        pltpu.SMEM((N,), F32), pltpu.VMEM((1, N), jnp.int32), pltpu.VMEM((1, N), jnp.int32), vm(2, N, N),
        vm(34, 16, N), vm(2, 32, N), vm(3, 32, 16, N), vm(34, 16, N), vm(3, N, N), pltpu.VMEM((N, N), BF16), pltpu.VMEM((384, N), BF16),
        pltpu.VMEM((2, N, N), BF16), pltpu.VMEM((2, N, N), BF16), pltpu.VMEM((512, N), BF16), vm(N, 128),
        vm(4, N, 128), vm(N, 1024), vm(2, 32, N), vm(2, 32, N), vm(4, 8, N), vm(2, 40, N), vm(32, 16, N),
        vm(128, 8, 128), vm(128, 8, 128), vm(512, N), vm(128, 8, 128), vm(128, 8, 128), vm(2, 32, N),
        vm(4, 128, 7, 128), vm(4, 128, 7, 128), vm(128, 1, 128), vm(128, 1, 128), pltpu.VMEM((4, 128, N), BF16),
        vm(8, 128, 128), vm(10, 10, 8, 128),
        vm(5, 8, 8, 8, 128), vm(5, 8, 8, 8, 128), vm(5, 8, 8, 8, 128),
        vm(12, 2, 12, 16, 128), vm(12, 192, N), vm(8, 192, 384), vm(36, 24, N),
        vm(2, 2, 24, N), vm(2, 2, 32, N), vm(2, 2, 32, N), vm(4, 2, 8, N),
        dma((8,)), dma((8,)), dma((8,)), dma((4,)), dma((4,)), dma((8,)), dma((8,)),
        dma, dma, dma, dma, dma((4,)), dma((4,)), dma, dma,
    ]
    vmem = pl.BlockSpec(memory_space=pltpu.VMEM)
    hbm = pl.BlockSpec(memory_space=pl.ANY)
    disp, dens = pl.pallas_call(
        whole_kernel,
        out_shape=[sds(3, 32, 16, N), sds(32, 16, N)],
        in_specs=[hbm] * 7,
        out_specs=[hbm, vmem],
        scratch_shapes=scratch,
        compiler_params=pltpu.CompilerParams(vmem_limit_bytes=VLIM, collective_id=0, has_side_effects=True),
    )(
        jnp.asarray(LAP), owner.reshape(1, 256), window.reshape(1, 256), potential, jnp.asarray(TABLES),
        jnp.asarray(SELECT, BF16), jnp.asarray(SPREAD, BF16),
    )
    return pl.pallas_call(
        finish_kernel,
        out_shape=[sds(3, 32, 16, N), sds(32, 16, N)],
        in_specs=[hbm, hbm],
        out_specs=[hbm, hbm],
        scratch_shapes=[vm(4, 32, 16, N), dma((4, 2)), dma((4, 2))],
        compiler_params=pltpu.CompilerParams(vmem_limit_bytes=VLIM),
    )(disp, dens)


def solution(mesh):
    return jax.shard_map(
        per_device,
        mesh=mesh,
        in_specs=(P("px", "py", None), P("px", "py", None, None), P("px", "py", None)),
        out_specs=(P(None, "px", "py", None), P("px", "py", None)),
        check_vma=False,
    )
```

```python
import functools
import math

import jax
import jax.numpy as jnp
import numpy as np
from jax import lax
from jax.experimental import pallas as pl
from jax.experimental.pallas import tpu as pltpu
from jax.sharding import PartitionSpec as P

SECOND_ORDER = 3.0 / 7.0
HIGHEST = lax.Precision.HIGHEST
F32 = jnp.float32
BF16 = jnp.bfloat16
N = 256
VLIM = 60 * 1024 * 1024


def cas_table(a, b):
    angle = (np.multiply.outer(a, b) % N) * (2.0 * math.pi / N)
    return np.cos(angle) + np.sin(angle)


def constants():
    n = np.arange(N)
    r = np.arange(N)
    x = 32 * (r // 32) + 4 * (r % 8) + r // 8 % 4
    lap = -4.0 * np.sin(math.pi * n / N) ** 2
    tables = np.stack([cas_table(n, n), cas_table(x, x), lap[x][:, None] + lap[None, :]])
    return tables.astype(np.float32), lap.astype(np.float32)


def block_select():
    sel = np.zeros((128, 2, 128), np.float32)
    side = np.zeros((256, 8, 32), np.float32)
    for by in range(2):
        for a in range(8):
            for c in range(8):
                sel[a * 16 + 8 * by + c, by, a * 8 + c] = 1.0
            if by == 0:
                sel[a * 16 + 8, by, 88 + a] = 1.0
            else:
                sel[a * 16 + 7, by, 80 + a] = 1.0
        for bx in range(4):
            g = 2 * bx + by
            for c in range(8):
                side[bx * 32 + 8 * by + c, g, c] = 1.0
                side[bx * 32 + 16 + 8 * by + c, g, 8 + c] = 1.0
                side[(160 if by else 128) + bx * 8 + c, g, (24 if by else 16) + c] = 1.0
    return np.concatenate([sel.reshape(128, 256), side.reshape(256, 256)])


def spread_z():
    sel = np.zeros((12, 32, N), np.float32)
    for s in range(12):
        for b in range(32):
            sel[s, b, (8 * b + s - 2) % N] = 1.0
    return sel.reshape(384, N)


TABLES, LAP = constants()
SELECT = block_select()
SPREAD = spread_z()


def lane_iota(shape):
    return lax.broadcasted_iota(jnp.int32, shape, len(shape) - 1)


def swap_groups(vals, width):
    count = len(vals)
    group = lane_iota(vals[0].shape) // width
    turned = [pltpu.roll(v, k * width, 1) if k else v for k, v in enumerate(vals)]
    step = 1
    while step < count:
        high = (group & step) != 0
        turned = [jnp.where(high, turned[(k + step) % count], turned[k]) for k in range(count)]
        step *= 2
    return [pltpu.roll(turned[-k % count], 128 - k * width, 1) if k else turned[0] for k in range(count)]


def split3(x):
    a = x.astype(BF16)
    r = x - a.astype(F32)
    b = r.astype(BF16)
    c = (r - b.astype(F32)).astype(BF16)
    return a, b, c


def split2(x):
    a = x.astype(BF16)
    return a, (x - a.astype(F32)).astype(BF16)


def bdot(a, b):
    return jnp.dot(a, b, preferred_element_type=F32)


MESH = pl.DeviceIdType.MESH


def torus_rings():
    rings = [[] for _ in range(7)]
    for a in range(4):
        for b in range(4):
            for d in range(4):
                rings[sum(min(o, 4 - o) for o in (a, b, d))].append((a, b, d))
    return rings[::-1]


RINGS = torus_rings()
STEPS = ((1, 0), (-1, 0), (0, 1), (0, -1), (1, 1), (1, -1), (-1, 1), (-1, -1))
hdot = functools.partial(jnp.dot, precision=HIGHEST, preferred_element_type=F32)


def dot3(a, b):
    return bdot(a[0], b[0]) + (bdot(a[0], b[1]) + bdot(a[1], b[0]))


def rows_dot3(a, b):
    def one(x, y):
        return lax.dot_general(x, y, (((1,), (1,)), ((), ())), preferred_element_type=F32)

    return one(a[0], b[0]) + (one(a[0], b[1]) + one(a[1], b[0]))


def pair_halves(a, b):
    low = lane_iota(a.shape) < 64
    return jnp.where(low, a, pltpu.roll(b, 64, 1)), jnp.where(low, pltpu.roll(a, 64, 1), b)


def shift_rows(p, before, after):
    up = jnp.concatenate([p[1:], after], axis=0)
    down = jnp.concatenate([before, p[:-1]], axis=0)
    return up, down


def spline_taps(t):
    t = jnp.clip(t, -1.0, 1.0)
    up = jnp.maximum(t, 0.0)
    dn = up - t
    p3 = up * up * up * (1.0 / 6.0)
    n3 = dn * dn * dn * (1.0 / 6.0)
    sq = t * t
    both = p3 + n3
    base = sq * 0.5 + (1.0 / 6.0) - both
    half = t * 0.5
    return n3, base - half - 2.0 * n3, (2.0 / 3.0) - sq + 3.0 * both, base + half - 2.0 * p3, p3


def whole_kernel(
    lap_hbm, own_hbm, win_hbm, p_hbm, tab_hbm, sel_hbm, sp_hbm,
    disp_hbm, dens_ref,
    lap_ref, orow_ref, wrow_ref, inv_ref, phi, fyr, buf, pp, tab, sel_ref, sp_ref, tz, lx, hot_ref, wcol,
    ft_all, w_ref, pys, pyr, pcr, yl, src, a_out, a_in, m_ref, b_out, b_in, fys,
    c_out, c_in, l_out, l_in, named_ref, ct_ref, cp, wx_ref, wy_ref, wz_ref, d_ref, g_ref, h_ref, tile, rxr, rys, ryr, rcr,
    lsem, hss, hsr, fss, fsr, rss, rsr, ass, asr, bss, bsr, css, csr, qss, qsr,
):
    ix, iy = lax.axis_index("px"), lax.axis_index("py")
    me = ix * 16 + iy
    barrier = pltpu.get_barrier_semaphore()

    cx, core, cy, cz = ix // 2, lax.rem(ix, 2), iy // 4, lax.rem(iy, 4)

    def each_peer(act):
        for offsets in RINGS:

            def ring(n, carry, offsets=offsets):
                side = lax.rem(core + n + 1, 2)
                for a, b, d in offsets:
                    act(lax.rem(cx + a, 4) * 2 + side, lax.rem(cy + b, 4) * 4 + lax.rem(cz + d, 4))
                return carry

            lax.fori_loop(0, 2 if offsets[0] != (0, 0, 0) else 1, ring, 0)

    def greet(px, py):
        pl.semaphore_signal(barrier, 1, device_id=(px, py), device_id_type=MESH)

    each_peer(greet)

    def near(k, source, dest, ssem, rsem):
        dx, dy = STEPS[k]
        where = (lax.rem(ix + dx + 8, 8), lax.rem(iy + dy + 16, 16))
        copy = pltpu.make_async_remote_copy(
            source, dest, ssem.at[k], rsem.at[k], device_id=where, device_id_type=MESH
        )
        copy.start()
        return copy

    def scatter(out, into, ssem, rsem):
        def send(px, py):
            pltpu.make_async_remote_copy(
                out.at[px * 16 + py], into.at[me], ssem, rsem, device_id=(px, py), device_id_type=MESH
            ).start()

        each_peer(send)
        into[me] = out[me]

    def settle(out, into, sem):
        pltpu.make_async_copy(out.at[pl.ds(0, 127)], into.at[pl.ds(0, 127)], sem).wait()

    loads = [
        pltpu.make_async_copy(p_hbm, pp.at[pl.ds(1, 32)], lsem.at[0]),
        pltpu.make_async_copy(tab_hbm, tab, lsem.at[1]),
        pltpu.make_async_copy(sel_hbm, sel_ref, lsem.at[2]),
        pltpu.make_async_copy(sp_hbm, sp_ref, lsem.at[3]),
        pltpu.make_async_copy(lap_hbm, lap_ref, lsem.at[5]),
        pltpu.make_async_copy(own_hbm, orow_ref, lsem.at[6]),
        pltpu.make_async_copy(win_hbm, wrow_ref, lsem.at[7]),
    ]
    for load in loads:
        load.start()
    loads[0].wait()
    pys[0] = pp[1:33, 15, :]
    pys[1] = pp[1:33, 0, :]
    pl.semaphore_wait(barrier, 127)
    copies = [
        near(0, pp.at[32], pp.at[0], hss, hsr),
        near(1, pp.at[1], pp.at[33], hss, hsr),
        near(2, pys.at[0], pyr.at[0], hss, hsr),
        near(3, pys.at[1], pyr.at[1], hss, hsr),
        near(4, pp.at[32, pl.ds(8, 8)], pcr.at[0], hss, hsr),
        near(5, pp.at[32, pl.ds(0, 8)], pcr.at[1], hss, hsr),
        near(6, pp.at[1, pl.ds(8, 8)], pcr.at[2], hss, hsr),
        near(7, pp.at[1, pl.ds(0, 8)], pcr.at[3], hss, hsr),
    ]
    loads[1].wait()
    tz[0], tz[1] = split2(tab[0])
    lx[0], lx[1] = split2(tab[1])
    for copy in copies:
        copy.wait()
    yl[0, 0:1] = pcr[0, 7:8]
    yl[0, 1:33] = pyr[0]
    yl[0, 33:34] = pcr[2, 7:8]
    yl[1, 0:1] = pcr[1, 0:1]
    yl[1, 1:33] = pyr[1]
    yl[1, 33:34] = pcr[3, 0:1]

    planes = []
    for x in range(34):
        p = pp[x]
        up, down = shift_rows(p, yl[0, x : x + 1], yl[1, x : x + 1])
        ahead, behind = pltpu.roll(p, N - 1, 1), pltpu.roll(p, 1, 1)
        planes.append((p, up - down, ahead - behind, up + down - 2.0 * p, ahead + behind - 2.0 * p))
        if x < 2:
            continue
        (p0, dy0, dz0, _, _), (p1, dy1, _, yy, zz), (p2, dy2, dz2, _, _) = planes[-3:]
        xx = p2 - 2.0 * p1 + p0
        xy, xz = dy2 - dy0, dz2 - dz0
        yz = pltpu.roll(dy1, N - 1, 1) - pltpu.roll(dy1, 1, 1)
        src[x - 2] = xx * (yy + zz) + yy * zz - (xy * xy + xz * xz + yz * yz) * 0.0625
        if x % 8 == 1:
            h = x // 8 - 1
            part = split2(src[8 * h : 8 * h + 8].reshape(128, N))
            r = rows_dot3((tz[0], tz[1]), part)
            a_out[:, 2 * h, :], a_out[:, 2 * h + 1, :] = pair_halves(r[:128], r[128:])
    scatter(a_out, a_in, ass, asr)
    for load in loads[4:]:
        load.wait()
    wide = jnp.broadcast_to(orow_ref[...].astype(F32), (256, 256))
    r_i = lax.broadcasted_iota(jnp.int32, (256, 256), 0)
    c_i = lax.broadcasted_iota(jnp.int32, (256, 256), 1)
    same = jnp.where((wide.T == wide) & (r_i < c_i), 1, 0)
    slot = jnp.sum(same, axis=0, keepdims=True) * 128 + orow_ref[...]
    hot_ref[...] = (lax.broadcasted_iota(jnp.int32, (512, 256), 0) == slot).astype(F32).astype(BF16)
    wcol[...] = jnp.broadcast_to(wrow_ref[...].astype(F32) + 1.0, (128, 256)).T
    quarter = lane_iota((128, 128)) // 32
    names = 0.0
    for r in range(4):
        picked = bdot(hot_ref[128 * r : 128 * r + 128], wcol[...].astype(BF16))
        names = names + jnp.where(quarter == r, picked, 0.0)
    l_out[...] = names.reshape(128, 1, 128)
    scatter(l_out, l_in, qss, qsr)
    scale = SECOND_ORDER / (N * N * N)
    for q in range(2):
        eigen = tab[2] + lap_ref[me + 128 * q]
        anchor = eigen == 0.0
        inv_ref[q] = jnp.where(anchor, 0.0, scale / jnp.where(anchor, -1.0, eigen))
    settle(a_out, a_in, asr)

    for i in range(8):
        for h in range(2):
            vals = swap_groups([a_in[i * 16 + h * 8 + k] for k in range(8)], 16)
            for k in range(8):
                row = (k // 4) * 256 + i * 32 + (k % 4) * 8
                m_ref[row : row + 8, 128 * h : 128 * h + 128] = vals[k]
    tzs, lxs = (tz[0], tz[1]), (lx[0], lx[1])
    b = dot3(split2(m_ref[...]), tzs)
    halves = []
    for q in range(2):
        c = dot3(lxs, split2(b[256 * q : 256 * q + 256]))
        c = c * inv_ref[q]
        halves.append(hdot(tab[1], c))
    m_ref[...] = hdot(jnp.concatenate(halves, axis=0), tab[0])
    for i in range(8):
        for h in range(2):
            vals = []
            for k in range(8):
                row = (k // 4) * 256 + i * 32 + (k % 4) * 8
                vals.append(m_ref[row : row + 8, 128 * h : 128 * h + 128])
            vals = swap_groups(vals, 16)
            for k in range(8):
                b_out[i * 16 + h * 8 + k] = vals[k]
    scatter(b_out, b_in, bss, bsr)
    settle(b_out, b_in, bsr)
    for h in range(4):
        a = jnp.concatenate(pair_halves(b_in[:, 2 * h, :], b_in[:, 2 * h + 1, :]), axis=0)
        phi[8 * h + 1 : 8 * h + 9] = pp[8 * h + 1 : 8 * h + 9] + hdot(a.T, tab[0]).reshape(8, 16, N)
    fys[0] = phi[1:33, 15, :]
    fys[1] = phi[1:33, 0, :]
    copies = [
        near(0, phi.at[32], phi.at[0], fss, fsr),
        near(1, phi.at[1], phi.at[33], fss, fsr),
        near(2, fys.at[0], fyr.at[0], fss, fsr),
        near(3, fys.at[1], fyr.at[1], fss, fsr),
    ]
    loads[2].wait()
    loads[3].wait()

    def chosen(ft, sel):
        out = 0.0
        for part in split3(jnp.concatenate([ft[pl.ds(e, 32, stride=8), :] for e in range(8)], axis=0)):
            out = out + bdot(part, sel)
        return out

    for m in range(4):
        ft_all[m] = phi[8 * m + 1 : 8 * m + 9].reshape(128, N).T
        w_ref[:, 256 * m : 256 * m + 256] = chosen(ft_all.at[m], sel_ref[0:128])
    for copy in copies:
        copy.wait()
    edge = [phi[8 * m + k] for m in range(4) for k in (0, 9)]
    ft_all[0] = jnp.concatenate(edge, axis=0).T
    ft_all[1] = jnp.concatenate([fyr[0], fyr[1], jnp.zeros((64, N), F32)], axis=0).T
    edge = jnp.concatenate(
        [jnp.concatenate([ft_all[m, pl.ds(e, 32, stride=8), :] for e in range(8)], axis=0) for m in range(2)], axis=1
    )
    rim = 0.0
    for part in split3(edge):
        rim = rim + bdot(part, sel_ref[128:384])
    lanes = lane_iota((256, 128))
    inner = (lanes >= 64) & (lanes < 96)
    w = []
    for g in range(8):
        turned = rim[:, 128 * (g // 4) : 128 * (g // 4) + 128]
        if g % 4 != 2:
            turned = pltpu.roll(turned, (192 - 32 * (g % 4)) % 128, 1)
        w.append(w_ref[:, 128 * g : 128 * g + 128] + jnp.where(inner, turned, 0.0))
    w = jnp.concatenate(w, axis=1)

    def slab(e, turn):
        rows = w[32 * e : 32 * e + 32]
        if turn:
            rows = pltpu.roll(rows, turn, 0)
        return jnp.concatenate([rows[:, 128 * g : 128 * g + 128] for g in range(8)], axis=0)

    zfaces = (slab(7, 1), slab(0, 31))
    hot = hot_ref[...]

    def full(k):
        face = pltpu.roll(zfaces[k // 4], 96 - 16 * (k % 4), 1)
        return jnp.where(lanes >= 96, face, slab(k, 0))

    last = full(7)
    parts = []
    for e in range(0, 7, 2):
        pair = []
        for k in range(e, min(e + 2, 7)):
            tail = pltpu.roll(last, 112 - 16 * k, 1)
            pair.append(jnp.where(lanes >= 112, tail, full(k)))
        parts.append(split3(jnp.concatenate(pair, axis=1)))

    def place(first, count):
        rows = hot[128 * first : 128 * (first + count)]
        for k, (a, b, c) in enumerate(parts):
            o = bdot(rows, a) + bdot(rows, b) + bdot(rows, c)
            for r in range(count):
                c_out[first + r, :, 2 * k, :] = o[128 * r : 128 * r + 128, :128]
                if k < 3:
                    c_out[first + r, :, 2 * k + 1, :] = o[128 * r : 128 * r + 128, 128:]

    place(0, 1)
    scatter(c_out.at[0], c_in.at[0], css.at[0], csr.at[0])
    place(1, 3)
    scatter(c_out.at[1], c_in.at[1], css.at[1], csr.at[1])
    settle(l_out, l_in, qsr)
    ids = lane_iota((128, 256)).astype(F32) + 1.0
    for r in range(4):
        label = l_in[...].reshape(128, 128)[:, 32 * r : 32 * r + 1]
        named_ref[r] = (jnp.broadcast_to(label, (128, 256)) == ids).astype(F32).astype(BF16)
    scatter(c_out.at[2], c_in.at[2], css.at[2], csr.at[2])
    for x in range(32):
        f = phi[x + 1]
        up, down = shift_rows(f, fyr[0, x : x + 1], fyr[1, x : x + 1])
        buf[0, x] = (phi[x] - phi[x + 2]) * 0.5
        buf[1, x] = (down - up) * 0.5
        buf[2, x] = (pltpu.roll(f, 1, 1) - pltpu.roll(f, N - 1, 1)) * 0.5
    stored = pltpu.make_async_copy(buf, disp_hbm, lsem.at[4])
    stored.start()
    scatter(c_out.at[3], c_in.at[3], css.at[3], csr.at[3])
    sub = lax.broadcasted_iota(jnp.int32, (8, 8, 128), 1)
    sub5 = lax.broadcasted_iota(jnp.int32, (8, 128), 0)

    def chunk(r, slot):
        settle(c_out.at[r], c_in.at[r], csr.at[r])

        for e in range(7):
            ct_ref[e] = c_in[r, :, e, :].T
            ct_ref[7, 16 * e : 16 * e + 16] = ct_ref[e, 112:128]
        for e in range(8):
            cp[e + 1, 1:9] = ct_ref[e, 0:64].reshape(8, 8, 128)
            cp[e + 1, 0] = ct_ref[e, 64:72]
            cp[e + 1, 9] = ct_ref[e, 72:80]
            k = 1 + 2 * (e % 4)
            cp[9 * (e // 4), k : k + 2] = ct_ref[e, 96:112].reshape(2, 8, 128)

        def taps(e, carry):
            f = cp[e + 1, 1:9]
            ym = jnp.stack([jnp.broadcast_to(ct_ref[e, 80 + k : 81 + k], (8, 128)) for k in range(8)])
            yp = jnp.stack([jnp.broadcast_to(ct_ref[e, 88 + k : 89 + k], (8, 128)) for k in range(8)])
            ym = jnp.where(sub == 0, ym, pltpu.roll(f, 1, 1))
            yp = jnp.where(sub == 7, yp, pltpu.roll(f, 7, 1))
            triples = (
                (wx_ref, cp[e + 1, 0:8], cp[e + 1, 2:10]),
                (wy_ref, ym, yp),
                (wz_ref, cp[e, 1:9], cp[e + 2, 1:9]),
            )
            for ref, lo, hi in triples:
                for d, tap in enumerate(spline_taps((lo - hi) * 0.5)):
                    ref[d, e] = tap
            return carry

        lax.fori_loop(0, 8, taps, 0)
        for u in range(12):
            acc = [None] * 12
            for e in range(8):
                for a in range(max(0, u - 4), min(8, u + 1)):
                    q = wx_ref[u - a, e, a][None] * wy_ref[:, e, a]
                    for dz in range(5):
                        v = q * wz_ref[dz, e, a][None]
                        k = e + dz
                        acc[k] = v if acc[k] is None else acc[k] + v
                for k in [e] if e < 7 else range(7, 12):
                    turned = [pltpu.roll(acc[k][dy], dy, 0) for dy in range(1, 5)]
                    over = [jnp.where(sub5 < dy, t, 0.0) for dy, t in enumerate(turned, 1)]
                    hi = (over[0] + over[1]) + (over[2] + over[3])
                    d_ref[k, slot, u, 0:8, :] = acc[k][0] + (turned[0] + turned[1]) + (turned[2] + turned[3]) - hi
                    d_ref[k, slot, u, 8:16, :] = hi

    def pair(n, carry):
        for r in range(2):
            chunk(2 * n + r, r)
        named = jnp.concatenate([named_ref[2 * n], named_ref[2 * n + 1]], axis=0)
        for k in range(12):
            a, b = split2(jnp.concatenate([d_ref[k, r].reshape(192, 128) for r in range(2)], axis=1))
            g_ref[k] = g_ref[k] + (bdot(a, named) + bdot(b, named))
        return carry

    g_ref[...] = jnp.zeros_like(g_ref)
    lax.fori_loop(0, 2, pair, 0)
    for half in range(2):
        for k in range(3):
            vals = [g_ref[4 * k + m][:, 128 * half : 128 * half + 128] for m in range(4)]
            vals = swap_groups(vals, 32)
            for gl in range(4):
                h_ref[half * 4 + gl, :, 128 * k : 128 * k + 128] = vals[gl]
    tile[...] = jnp.zeros_like(tile)
    sp = sp_ref[...]
    for g in range(8):
        a, b = split2(h_ref[g])
        o = (bdot(a, sp) + bdot(b, sp)).reshape(12, 16, N)
        bx, by = g // 2, g % 2
        tile[8 * bx : 8 * bx + 12, 8 * by : 8 * by + 16, :] += o
    for k in range(2):
        rys[0, k] = tile[2:34, 18 + k, :]
        rys[1, k] = tile[2:34, k, :]
    copies = [
        near(0, tile.at[pl.ds(34, 2)], rxr.at[0], rss, rsr),
        near(1, tile.at[pl.ds(0, 2)], rxr.at[1], rss, rsr),
        near(2, rys.at[0], ryr.at[0], rss, rsr),
        near(3, rys.at[1], ryr.at[1], rss, rsr),
        near(4, tile.at[pl.ds(34, 2), pl.ds(16, 8)], rcr.at[0], rss, rsr),
        near(5, tile.at[pl.ds(34, 2), pl.ds(0, 8)], rcr.at[1], rss, rsr),
        near(6, tile.at[pl.ds(0, 2), pl.ds(16, 8)], rcr.at[2], rss, rsr),
        near(7, tile.at[pl.ds(0, 2), pl.ds(0, 8)], rcr.at[3], rss, rsr),
    ]
    dens_ref[...] = tile[2:34, 2:18, :]
    for copy in copies:
        copy.wait()
    dens_ref[0:2] += rxr[0, :, 2:18, :]
    dens_ref[30:32] += rxr[1, :, 2:18, :]
    for k in range(2):
        dens_ref[:, k, :] += ryr[0, k]
        dens_ref[:, 14 + k, :] += ryr[1, k]
    dens_ref[0:2, 0:2] += rcr[0, :, 2:4]
    dens_ref[0:2, 14:16] += rcr[1, :, 0:2]
    dens_ref[30:32, 0:2] += rcr[2, :, 2:4]
    dens_ref[30:32, 14:16] += rcr[3, :, 0:2]
    stored.wait()
    settle(a_out, a_in, ass)
    settle(l_out, l_in, qss)
    settle(b_out, b_in, bss)
    for r in range(4):
        settle(c_out.at[r], c_in.at[r], css.at[r])


def finish_kernel(disp, dens, disp_out, dens_out, buf, isem, osem):
    into, out = [], []
    for g in range(4):
        part = pl.ds(8 * g, 8)
        slots = buf.at[:, part]
        into.append(pltpu.make_async_copy(disp.at[:, part], slots.at[0:3], isem.at[g, 0]))
        into.append(pltpu.make_async_copy(dens.at[part], slots.at[3], isem.at[g, 1]))
        out.append(pltpu.make_async_copy(slots.at[0:3], disp_out.at[:, part], osem.at[g, 0]))
        out.append(pltpu.make_async_copy(slots.at[3], dens_out.at[part], osem.at[g, 1]))
    for copy in into:
        copy.start()
    for a, b in zip(into, out):
        a.wait()
        b.start()
    for copy in out:
        copy.wait()


def vm(*shape):
    return pltpu.VMEM(shape, F32)


def sds(*shape):
    return jax.ShapeDtypeStruct(shape, F32)


def per_device(potential, owner, window):
    dma = pltpu.SemaphoreType.DMA
    scratch = [
        pltpu.SMEM((N,), F32), pltpu.VMEM((1, N), jnp.int32), pltpu.VMEM((1, N), jnp.int32), vm(2, N, N),
        vm(34, 16, N), vm(2, 32, N), vm(3, 32, 16, N), vm(34, 16, N), vm(3, N, N), pltpu.VMEM((384, N), BF16), pltpu.VMEM((384, N), BF16),
        pltpu.VMEM((2, N, N), BF16), pltpu.VMEM((2, N, N), BF16), pltpu.VMEM((512, N), BF16), vm(N, 128),
        vm(4, N, 128), vm(N, 1024), vm(2, 32, N), vm(2, 32, N), vm(4, 8, N), vm(2, 40, N), vm(32, 16, N),
        vm(128, 8, 128), vm(128, 8, 128), vm(512, N), vm(128, 8, 128), vm(128, 8, 128), vm(2, 32, N),
        vm(4, 128, 7, 128), vm(4, 128, 7, 128), vm(128, 1, 128), vm(128, 1, 128), pltpu.VMEM((4, 128, N), BF16),
        vm(8, 128, 128), vm(10, 10, 8, 128),
        vm(5, 8, 8, 8, 128), vm(5, 8, 8, 8, 128), vm(5, 8, 8, 8, 128),
        vm(12, 2, 12, 16, 128), vm(12, 192, N), vm(8, 192, 384), vm(36, 24, N),
        vm(2, 2, 24, N), vm(2, 2, 32, N), vm(2, 2, 32, N), vm(4, 2, 8, N),
        dma((8,)), dma((8,)), dma((8,)), dma((4,)), dma((4,)), dma((8,)), dma((8,)),
        dma, dma, dma, dma, dma((4,)), dma((4,)), dma, dma,
    ]
    vmem = pl.BlockSpec(memory_space=pltpu.VMEM)
    hbm = pl.BlockSpec(memory_space=pl.ANY)
    disp, dens = pl.pallas_call(
        whole_kernel,
        out_shape=[sds(3, 32, 16, N), sds(32, 16, N)],
        in_specs=[hbm] * 7,
        out_specs=[hbm, vmem],
        scratch_shapes=scratch,
        compiler_params=pltpu.CompilerParams(vmem_limit_bytes=VLIM, collective_id=0, has_side_effects=True),
    )(
        jnp.asarray(LAP), owner.reshape(1, 256), window.reshape(1, 256), potential, jnp.asarray(TABLES),
        jnp.asarray(SELECT, BF16), jnp.asarray(SPREAD, BF16),
    )
    return pl.pallas_call(
        finish_kernel,
        out_shape=[sds(3, 32, 16, N), sds(32, 16, N)],
        in_specs=[hbm, hbm],
        out_specs=[hbm, hbm],
        scratch_shapes=[vm(4, 32, 16, N), dma((4, 2)), dma((4, 2))],
        compiler_params=pltpu.CompilerParams(vmem_limit_bytes=VLIM),
    )(disp, dens)


def solution(mesh):
    return jax.shard_map(
        per_device,
        mesh=mesh,
        in_specs=(P("px", "py", None), P("px", "py", None, None), P("px", "py", None)),
        out_specs=(P(None, "px", "py", None), P("px", "py", None)),
        check_vma=False,
    )
```
